128 devices in a mesh: dp: 2 (over z_lo), head: 8 (over z_hi, y), tensor: 8 (over x, core).
Axes of the slice: x: 4, y: 4, z: 4 (z_hi: 2, z_lo: 2; z = z_hi * 2 + z_lo), core: 2. Of those that a mesh axis runs over, the one named last changes fastest.
Arguments:
- tokens: bfloat16 [512, 8192], P('dp', 'tensor'), may hold values from -6 to 6
- cotangent: bfloat16 [512, 8192], P('dp', 'tensor'), may hold values from -6 to 6
- w_gate: bfloat16 [8192, 29568], P('tensor', 'head'), may hold values from -0.0625 to 0.0625
- w_up: bfloat16 [8192, 29568], P('tensor', 'head'), may hold values from -0.0625 to 0.0625
- w_down: bfloat16 [29568, 8192], P('head', 'tensor'), may hold values from -0.03125 to 0.03125
- common_down_factor: bfloat16 [8192, 64], P('tensor'), may hold values from -0.0625 to 0.0625
- head_up: bfloat16 [64, 64, 8192], P('head', None, 'tensor'), may hold values from -0.0625 to 0.0625
- routes: int32 [512, 1], P('dp'), may hold values from 0 to 63
Outputs:
- grad_x: bfloat16 [512, 8192], P(('dp', 'head'), 'tensor')
- grad_shared: float32 [8192, 64], P('tensor')
- up_head_gradients: float32 [64, 64, 8192], P('head', None, 'tensor')
The draws below stay inside these ranges and needn't reach their ends.
Inputs may be any that keep to these rules, and one draw needn't show every extreme that they name: `routes`: each token names one adapter head; the loads are skewed.
All inputs are finite; a program needn't handle non-finite values.
Results may differ from the reference program's by a relative error of at most 0.015.
Values may be sent and summed in bfloat16 or wider, within the bound.
A program may use at most 128 MiB of HBM per device.

```python
import jax
import jax.numpy as jnp
from jax import lax

MODEL_WIDTH = 8192
FF = 29568
ADAPTER_RANK = 64
UP_HEADS = 64
TOKEN_TOTAL = 512


def levels(key, extent, split, smallest, top_value):
    loudness, own = 1.0, jax.random.fold_in(key, 6)
    for axis_at, blocks in split:
        steps = jnp.exp(jax.random.uniform(jax.random.fold_in(own, axis_at), (blocks,), jnp.float32, smallest / len(split), top_value / len(split)))
        loudness = loudness * jnp.repeat(steps, extent[axis_at] // blocks).reshape([-1 if axis == axis_at else 1 for axis in range(len(extent))])
    return loudness


def choose_distinct(stream_key, rows, number_of, top, lift):
    ranking = jax.random.permutation(jax.random.fold_in(stream_key, 1), number_of)
    boost = ranking
    for power in range(3):
        boost = boost * boost // number_of
    boost = boost * lift // number_of
    lots = jax.random.randint(jax.random.fold_in(stream_key, 2), (rows, number_of), 0, 4096) + boost
    sure = jax.random.permutation(jax.random.fold_in(stream_key, 3), rows)[jnp.arange(number_of) % rows]
    lots = jnp.where(jnp.arange(rows)[:, None] == sure[None, :], 1 << 14, lots)
    merit = lots * number_of + jnp.arange(number_of)
    return lax.top_k(merit.astype(jnp.int32), top)[1].astype(jnp.int32)


def gaussian(rng, shape, scale, most, split=(), held_as=jnp.bfloat16):
    result = jax.random.normal(rng, shape, jnp.float32) * scale
    if len(split) > 0:
        result = levels(rng, shape, split, -0.22, 0.18) * result
    return jnp.clip(result, min=-most, max=most).astype(held_as)


def setup_inputs(seed: int = 0) -> dict:
    keys = jax.random.split(jax.random.key(seed), 9)
    tokens = gaussian(keys[0], (TOKEN_TOTAL, MODEL_WIDTH), 1.0, 6.0, ((0, 2), (1, 8)))
    cotangent = gaussian(keys[1], (TOKEN_TOTAL, MODEL_WIDTH), 1.0, 6.0, ((0, 2), (1, 8)))
    w_gate = gaussian(keys[2], (MODEL_WIDTH, FF), MODEL_WIDTH ** -0.5, 0.0625, ((0, 8), (1, 8)))
    w_up = gaussian(keys[3], (MODEL_WIDTH, FF), MODEL_WIDTH ** -0.5, 0.0625, ((0, 8), (1, 8)))
    w_down = gaussian(keys[4], (FF, MODEL_WIDTH), FF ** -0.5, 0.03125, ((0, 8), (1, 8)))
    common_down_factor = gaussian(keys[5], (MODEL_WIDTH, ADAPTER_RANK), MODEL_WIDTH ** -0.5, 0.0625, ((0, 8),))
    head_up = gaussian(keys[6], (UP_HEADS, ADAPTER_RANK, MODEL_WIDTH), MODEL_WIDTH ** -0.5, 0.0625, ((0, 8), (2, 8)))
    routes = choose_distinct(keys[7], TOKEN_TOTAL, UP_HEADS, 1, 256)
    return {"tokens": tokens, "cotangent": cotangent, "w_gate": w_gate, "w_up": w_up, "w_down": w_down, "common_down_factor": common_down_factor, "head_up": head_up, "routes": routes}


ADAPTER_SCALE = 2.0


def reference(tokens, cotangent, w_gate, w_up, w_down, common_down_factor, head_up, routes):
    gate_preactivation = jnp.dot(tokens, w_gate, preferred_element_type=jnp.float32)
    up_preactivation = jnp.dot(tokens, w_up, preferred_element_type=jnp.float32)
    returned_gradient = jnp.dot(cotangent, w_down.T, preferred_element_type=jnp.float32)
    adapter_selectors = jnp.dot(tokens, common_down_factor, preferred_element_type=jnp.float32).astype(jnp.bfloat16)
    indicator_matrix = (routes == jnp.arange(UP_HEADS, dtype=jnp.int32)[None, :]).astype(jnp.float32)
    head_separated = jnp.dot(cotangent, head_up.reshape(UP_HEADS * ADAPTER_RANK, MODEL_WIDTH).T, preferred_element_type=jnp.float32)
    selector_gradient = (ADAPTER_SCALE * jnp.sum(head_separated.reshape(TOKEN_TOTAL, UP_HEADS, ADAPTER_RANK) * indicator_matrix[:, :, None], axis=1)).astype(jnp.bfloat16)
    sig_gate = jax.nn.sigmoid(gate_preactivation)
    gate_gradient = (returned_gradient * up_preactivation * sig_gate * (1.0 + gate_preactivation * (1.0 - sig_gate))).astype(jnp.bfloat16)
    up_gradient = (returned_gradient * gate_preactivation * sig_gate).astype(jnp.bfloat16)
    grad_x = (jnp.dot(gate_gradient, w_gate.T, preferred_element_type=jnp.float32)
              + jnp.dot(up_gradient, w_up.T, preferred_element_type=jnp.float32)
              + jnp.dot(selector_gradient, common_down_factor.T, preferred_element_type=jnp.float32)).astype(jnp.bfloat16)
    selector_mask = (adapter_selectors.astype(jnp.float32)[:, None, :] * indicator_matrix[:, :, None]).astype(jnp.bfloat16).reshape(TOKEN_TOTAL, UP_HEADS * ADAPTER_RANK)
    up_head_gradients = (ADAPTER_SCALE * jnp.dot(selector_mask.T, cotangent, preferred_element_type=jnp.float32)).reshape(UP_HEADS, ADAPTER_RANK, MODEL_WIDTH)
    grad_shared = jnp.dot(tokens.T, selector_gradient, preferred_element_type=jnp.float32)
    return grad_x, grad_shared, up_head_gradients
```

```python
import jax
import jax.numpy as jnp
from jax import lax
from jax.sharding import PartitionSpec as P

ADAPTER_SCALE = 2.0


def contract_last(left, right):
    return lax.dot_general(
        left, right, (((1,), (1,)), ((), ())), preferred_element_type=jnp.float32
    )


def local(tokens, cotangent, w_gate, w_up, w_down, common_down_factor, head_up, routes):
    tok_rows, d_cols = tokens.shape
    hidden_activation = w_gate.shape[1]
    reduced_activation = common_down_factor.shape[1]
    local_heads = head_up.shape[0]
    first_head = lax.axis_index("head") * local_heads
    assigned_mask = (
        routes == first_head + jnp.arange(local_heads, dtype=jnp.int32)[None, :]
    ).astype(jnp.float32)
    flat_heads = head_up.reshape(local_heads * reduced_activation, d_cols)
    gate_preactivation = jnp.dot(tokens, w_gate, preferred_element_type=jnp.float32)
    up_preactivation = jnp.dot(tokens, w_up, preferred_element_type=jnp.float32)
    returned_gradient = contract_last(cotangent, w_down)
    adapter_selectors = jnp.dot(tokens, common_down_factor, preferred_element_type=jnp.float32)
    head_separated = contract_last(cotangent, flat_heads).reshape(
        tok_rows, local_heads, reduced_activation
    )
    selector_gradient = ADAPTER_SCALE * jnp.sum(head_separated * assigned_mask[:, :, None], axis=1)
    partial = jnp.concatenate(
        [
            gate_preactivation.astype(jnp.bfloat16),
            up_preactivation.astype(jnp.bfloat16),
            returned_gradient.astype(jnp.bfloat16),
            adapter_selectors.astype(jnp.bfloat16),
            selector_gradient.astype(jnp.bfloat16),
        ],
        axis=1,
    )
    own_rows = lax.psum_scatter(partial, "tensor", scatter_dimension=0, tiled=True)
    gate_preactivation = own_rows[:, :hidden_activation].astype(jnp.float32)
    up_preactivation = own_rows[:, hidden_activation : 2 * hidden_activation].astype(jnp.float32)
    returned_gradient = own_rows[:, 2 * hidden_activation : 3 * hidden_activation].astype(
        jnp.float32
    )
    sig_gate = jax.nn.sigmoid(gate_preactivation)
    gate_gradient = (
        returned_gradient
        * up_preactivation
        * sig_gate
        * (1.0 + gate_preactivation * (1.0 - sig_gate))
    ).astype(jnp.bfloat16)
    up_gradient = (returned_gradient * gate_preactivation * sig_gate).astype(jnp.bfloat16)
    gathered = lax.all_gather(
        jnp.concatenate([gate_gradient, up_gradient, own_rows[:, 3 * hidden_activation :]], axis=1),
        "tensor",
        axis=0,
        tiled=True,
    )
    gate_gradient = gathered[:, :hidden_activation]
    up_gradient = gathered[:, hidden_activation : 2 * hidden_activation]
    adapter_selectors = gathered[
        :, 2 * hidden_activation : 2 * hidden_activation + reduced_activation
    ]
    selector_gradient = gathered[:, 2 * hidden_activation + reduced_activation :]
    ffn_part = (
        contract_last(gate_gradient, w_gate)
        + contract_last(up_gradient, w_up)
        + contract_last(selector_gradient, common_down_factor)
    )
    grad_x = lax.psum_scatter(
        ffn_part.astype(jnp.bfloat16), "head", scatter_dimension=0, tiled=True
    )
    selector_mask = (
        adapter_selectors[:, None, :] * assigned_mask[:, :, None].astype(jnp.bfloat16)
    ).reshape(tok_rows, local_heads * reduced_activation)
    head_contributions = ADAPTER_SCALE * lax.dot_general(
        selector_mask, cotangent, (((0,), (0,)), ((), ())), preferred_element_type=jnp.float32
    )
    up_head_gradients = lax.psum(
        head_contributions.reshape(local_heads, reduced_activation, d_cols).astype(jnp.bfloat16),
        "dp",
    ).astype(jnp.float32)
    shared_term = lax.dot_general(
        tokens, selector_gradient, (((0,), (0,)), ((), ())), preferred_element_type=jnp.float32
    )
    grad_shared = lax.psum(shared_term.astype(jnp.bfloat16), ("dp", "head")).astype(jnp.float32)
    return (grad_x, grad_shared, up_head_gradients)


def solution(mesh):
    placed = (
        P("dp", "tensor"),
        P("dp", "tensor"),
        P("tensor", "head"),
        P("tensor", "head"),
        P("head", "tensor"),
        P("tensor", None),
        P("head", None, "tensor"),
        P("dp", None),
    )
    return jax.shard_map(
        local,
        mesh=mesh,
        in_specs=placed,
        out_specs=(P(("dp", "head"), "tensor"), P("tensor", None), P("head", None, "tensor")),
        check_vma=False,
    )
```

```python
import jax
import jax.numpy as jnp
from jax import lax
from jax.experimental import pallas as pl
from jax.experimental.pallas import tpu as pltpu
from jax.sharding import PartitionSpec as P

ADAPTER_SCALE = 2.0
MESH = pl.DeviceIdType.MESH
F32, BF16 = jnp.float32, jnp.bfloat16
CHUNK = 512
TAIL = 128
LAG_ADD, LAG_RELAY, LAG_GRAD, LAG_FORWARD, LAG_LAST, LAG_BACK = 1, 2, 3, 4, 5, 6


class Box:
    pass


def nt(left, right):
    return lax.dot_general(left, right, (((1,), (1,)), ((), ())), preferred_element_type=F32)


def tn(left, right):
    return lax.dot_general(left, right, (((0,), (0,)), ((), ())), preferred_element_type=F32)


def body(names, nj, nh, *refs):
    r = Box()
    for name, ref in zip(names, refs):
        setattr(r, name, ref)
    hidden = nj * CHUNK
    tail = r.w_gate.shape[1] - hidden
    tau, h, dp = lax.axis_index("tensor"), lax.axis_index("head"), lax.axis_index("dp")
    x, c = tau // 2, lax.rem(tau, 2)
    step = 2 * c - 1
    xp, xm, x2 = lax.rem(x + step + 4, 4), lax.rem(x - step + 4, 4), lax.rem(x + 2, 4)
    sib = {"tensor": 2 * x + 1 - c}
    nxt, prv = {"tensor": 2 * xp + c}, {"tensor": 2 * xm + c}
    pair = {"dp": 1 - dp}

    def head_peer(k):
        return {"head": lax.rem(h + k, nh)}

    barrier = pltpu.get_barrier_semaphore()
    partners = [sib, nxt, prv, pair] + [head_peer(k) for k in range(1, nh)]
    for partner in partners:
        pl.semaphore_signal(barrier, inc=1, device_id=partner, device_id_type=MESH)

    def local(src, dst, sem):
        return pltpu.make_async_copy(src, dst, sem)

    def small_loads():
        return [
            local(r.tokens, r.tok, r.small_sem.at[0]),
            local(r.cotangent, r.cot, r.small_sem.at[1]),
            local(r.routes, r.rts, r.small_sem.at[2]),
            local(r.heads, r.hup, r.small_sem.at[3]),
            local(r.factor, r.cdf, r.small_sem.at[4]),
        ]

    def chunk_loads(j):
        cols = pl.ds(pl.multiple_of(j * CHUNK, CHUNK), CHUNK)
        return [
            local(r.w_gate.at[:, cols], r.wgu.at[j, :, pl.ds(0, CHUNK)], r.load_sem.at[j, 0]),
            local(r.w_up.at[:, cols], r.wgu.at[j, :, pl.ds(CHUNK, CHUNK)], r.load_sem.at[j, 1]),
            local(r.w_down.at[cols, :], r.wd.at[j], r.load_sem.at[j, 2]),
        ]

    def tail_loads():
        cols = pl.ds(hidden, tail)
        return [
            local(r.w_gate.at[:, cols], r.raw_g, r.small_sem.at[5]),
            local(r.w_up.at[:, cols], r.raw_u, r.small_sem.at[6]),
            local(r.w_down.at[cols, :], r.t_wd.at[pl.ds(0, tail), :], r.small_sem.at[7]),
        ]

    first = small_loads()
    first[0].start()
    for load in chunk_loads(0):
        load.start()
    for load in first[1:]:
        load.start()
    r.t_wg[...] = jnp.zeros_like(r.t_wg)
    r.t_wu[...] = jnp.zeros_like(r.t_wu)
    r.t_wd[...] = jnp.zeros_like(r.t_wd)
    for load in tail_loads():
        load.start()

    def start_chunk(j, carry):
        for load in chunk_loads(j):
            load.start()
        return carry

    lax.fori_loop(1, nj, start_chunk, 0)

    def main():
        b = Box()
        b.part, b.sibs = r.m_part, r.m_sibs
        b.s1, b.s2, b.s3, b.r1, b.r2, b.r3 = r.m_s1, r.m_s2, r.m_s3, r.m_r1, r.m_r2, r.m_r3
        b.grads, b.send, b.recv, b.width = r.m_grads, r.m_send, r.m_recv, CHUNK
        return b

    def special():
        b = Box()
        b.part, b.sibs = r.t_part, r.t_sibs
        b.s1, b.s2, b.s3, b.r1, b.r2, b.r3 = r.t_s1, r.t_s2, r.t_s3, r.t_r1, r.t_r2, r.t_r3
        b.grads, b.send, b.recv, b.width = r.t_grads, r.t_send, r.t_recv, TAIL
        return b

    main, special = main(), special()

    def remote(b, j, i, src, dst, to):
        return pltpu.make_async_remote_copy(
            src_ref=src,
            dst_ref=dst,
            send_sem=b.send.at[j, i],
            recv_sem=b.recv.at[j, i],
            device_id=to,
            device_id_type=MESH,
        )

    def to_sib(b, j):
        return remote(b, j, 0, b.part.at[j, 1 - c], b.sibs.at[j], sib)

    def sum_far(b, j):
        return remote(b, j, 1, b.s1.at[j], b.r1.at[j], nxt)

    def sum_near(b, j):
        return remote(b, j, 2, b.s2.at[j], b.r2.at[j], prv)

    def sum_on(b, j):
        return remote(b, j, 3, b.s3.at[j], b.r3.at[j], nxt)

    def grad(b, j, i, slot, to):
        return remote(b, j, i, b.grads.at[j, slot], b.grads.at[j, slot], to)

    own, far, near, ahead = 2 * x + c, 2 * x2 + c, 2 * xm + c, 2 * xp + c
    sib_own, sib_far, sib_near, sib_ahead = (
        2 * x + 1 - c,
        2 * x2 + 1 - c,
        2 * xm + 1 - c,
        2 * xp + 1 - c,
    )

    def add(b, j):
        to_sib(b, j).wait_recv()
        b.s1[j] = (b.part[j, c, x2].astype(F32) + b.sibs[j, x2].astype(F32)).astype(BF16)
        sum_far(b, j).start()
        b.s2[j] = (b.part[j, c, xm].astype(F32) + b.sibs[j, xm].astype(F32)).astype(BF16)
        sum_near(b, j).start()

    def relay(b, j):
        sum_far(b, j).wait_recv()
        b.s3[j] = (
            b.r1[j].astype(F32) + b.part[j, c, xp].astype(F32) + b.sibs[j, xp].astype(F32)
        ).astype(BF16)
        sum_on(b, j).start()

    def totals(b, j):
        sum_near(b, j).wait_recv()
        sum_on(b, j).wait_recv()
        width = b.width

        def part(lo, size):
            at = pl.ds(lo, size)
            return (
                b.r3[j, :, at].astype(F32)
                + b.r2[j, :, at].astype(F32)
                + b.part[j, c, x, :, at].astype(F32)
                + b.sibs[j, x, :, at].astype(F32)
            )

        gate, up, back = (part(i * width, width) for i in range(3))
        sig = jax.nn.sigmoid(gate)
        b.grads[j, own, :, pl.ds(0, width)] = (
            back * up * sig * (1.0 + gate * (1.0 - sig))
        ).astype(BF16)
        b.grads[j, own, :, pl.ds(width, width)] = (back * gate * sig).astype(BF16)
        return part

    def spread(b, j):
        grad(b, j, 4, own, nxt).start()
        grad(b, j, 5, own, prv).start()
        grad(b, j, 6, own, sib).start()

    def forward(b, j):
        grad(b, j, 4, near, nxt).wait_recv()
        grad(b, j, 7, near, nxt).start()
        grad(b, j, 8, near, sib).start()
        grad(b, j, 5, ahead, prv).wait_recv()
        grad(b, j, 9, ahead, sib).start()

    def last(b, j):
        grad(b, j, 7, far, nxt).wait_recv()
        grad(b, j, 10, far, sib).start()

    def arrived(b, j):
        grad(b, j, 6, sib_own, sib).wait_recv()
        grad(b, j, 8, sib_ahead, sib).wait_recv()
        grad(b, j, 9, sib_near, sib).wait_recv()
        grad(b, j, 10, sib_far, sib).wait_recv()

    def all_sent(b, j):
        for copy in (to_sib(b, j), sum_far(b, j), sum_near(b, j), sum_on(b, j)):
            copy.wait_send()
        grad(b, j, 4, own, nxt).wait_send()
        grad(b, j, 5, own, prv).wait_send()
        grad(b, j, 6, own, sib).wait_send()
        grad(b, j, 7, near, nxt).wait_send()
        grad(b, j, 8, near, sib).wait_send()
        grad(b, j, 9, ahead, sib).wait_send()
        grad(b, j, 10, far, sib).wait_send()

    def store_part(b, j, lo, value):
        for q in range(4):
            for core in range(2):
                at = (2 * q + core) * 32
                b.part[j, core, q, :, pl.ds(lo, value.shape[1])] = value[at : at + 32].astype(BF16)

    def other(i, src, dst, to):
        return pltpu.make_async_remote_copy(
            src_ref=src,
            dst_ref=dst,
            send_sem=r.o_send.at[i],
            recv_sem=r.o_recv.at[i],
            device_id=to,
            device_id_type=MESH,
        )

    def pair_cot():
        return other(0, r.cot, r.p_cot, pair)

    def pair_routes():
        return other(1, r.rb, r.p_rb, pair)

    def pair_codes():
        return other(2, r.codes, r.p_codes, pair)

    def pair_shared():
        return other(3, r.shared, r.p_shared, pair)

    def code_copy(k):
        return other(4 + k, r.mine, r.hx.at[k], head_peer(k))

    def x_copy(k):
        return other(4 + nh + k, r.xs.at[k], r.xr.at[k], head_peer(k))

    first_head = h * r.hup.shape[0]
    rank = r.cdf.shape[1]

    def lanes(shape):
        return lax.broadcasted_iota(jnp.int32, shape, 1)

    def special_matmuls():
        for load in small_loads()[2:] + tail_loads():
            load.wait()
        r.t_wg[:, pl.ds(0, tail)] = r.raw_g[...]
        r.t_wu[:, pl.ds(0, tail)] = r.raw_u[...]
        r.cdf2[...] = jnp.zeros_like(r.cdf2)
        r.cdf2[:, pl.ds(rank, rank)] = r.cdf[...]
        tok, cot = r.tok[...], r.cot[...]
        store_part(special, 0, 0, jnp.dot(tok, r.t_wg[...], preferred_element_type=F32))
        store_part(special, 0, TAIL, jnp.dot(tok, r.t_wu[...], preferred_element_type=F32))
        store_part(special, 0, 2 * TAIL, nt(cot, r.t_wd[...]))
        codes = jnp.dot(tok, r.cdf2[...], preferred_element_type=F32)
        routes = r.rts[...]
        r.rb[...] = jnp.broadcast_to(routes.astype(F32), r.rb.shape).astype(BF16)
        pair_routes().start()
        total = jnp.zeros_like(codes)
        half = (lanes(codes.shape) >= rank).astype(jnp.int32)
        for p in range(r.hup.shape[0] // 2):
            flat = jnp.concatenate([r.hup[2 * p], r.hup[2 * p + 1]], axis=0)
            total += jnp.where(routes == first_head + 2 * p + half, nt(cot, flat), 0.0)
        total = ADAPTER_SCALE * (total + pltpu.roll(total, rank, 1))
        store_part(special, 0, 3 * TAIL, jnp.where(half == 0, total, codes))

    def special_totals():
        part = totals(special, 0)
        r.mine[...] = part(3 * TAIL, TAIL).astype(BF16)
        for k in range(1, nh):
            code_copy(k).start()

    def special_spread():
        mine = r.mine[...].astype(F32)
        total = mine
        for k in range(1, nh):
            code_copy(k).wait_recv()
            total += r.hx[k].astype(F32)
        total = jnp.where(lanes(mine.shape) < rank, total, mine)
        special.grads[0, own, :, pl.ds(2 * TAIL, TAIL)] = total.astype(BF16)
        spread(special, 0)

    def up_heads(codes, routes, cot, fresh):
        both = jnp.where(
            lanes(codes.shape) < rank, pltpu.roll(codes.astype(F32), rank, 1), codes.astype(F32)
        )
        half = (lanes(codes.shape) >= rank).astype(F32)
        base = first_head.astype(F32) + half
        for p in range(r.hup.shape[0] // 2):
            chosen = jnp.where(routes.astype(F32) == base + 2.0 * p, both, 0.0).astype(BF16)
            grads = (ADAPTER_SCALE * tn(chosen, cot)).reshape(2, rank, cot.shape[1])
            if fresh:
                r.uph[pl.ds(2 * p, 2)] = grads
            else:
                r.o_heads[pl.ds(2 * p, 2)] = r.uph[pl.ds(2 * p, 2)] + grads

    def special_back():
        arrived(special, 0)
        grads = special.grads[0, :, :, pl.ds(0, 2 * TAIL)].reshape(256, 2 * TAIL)
        r.acc[...] = nt(grads[:, :TAIL], r.t_wg[...]) + nt(grads[:, TAIL:], r.t_wu[...])
        codes = special.grads[0, :, :, pl.ds(2 * TAIL, TAIL)].reshape(256, TAIL)
        r.codes[...] = codes
        pair_codes().start()
        r.shared[...] = tn(r.tok[...], codes)[:, :rank].astype(BF16)
        pair_shared().start()
        up_heads(codes, r.rb[...], r.cot[...], True)
        mine = special.grads[0, h, :, pl.ds(2 * TAIL, TAIL)]
        weights = jnp.where(lanes(r.cdf2.shape) < rank, pltpu.roll(r.cdf2[...].astype(F32), rank, 1), 0.0)
        r.xcode[...] = nt(mine, weights.astype(BF16))

    def special_pair():
        pair_cot().wait_recv()
        pair_routes().wait_recv()
        pair_codes().wait_recv()
        up_heads(r.p_codes[...], r.p_rb[...], r.p_cot[...], False)
        pair_shared().wait_recv()
        r.o_shared[...] = r.shared[...].astype(F32) + r.p_shared[...].astype(F32)

    def matmuls(j):
        loads = chunk_loads(j)
        loads[0].wait()
        tok = r.tok[...]
        store_part(main, j, 0, jnp.dot(tok, r.wgu[j, :, pl.ds(0, CHUNK)], preferred_element_type=F32))
        loads[1].wait()
        store_part(
            main, j, CHUNK, jnp.dot(tok, r.wgu[j, :, pl.ds(CHUNK, CHUNK)], preferred_element_type=F32)
        )
        loads[2].wait()
        store_part(main, j, 2 * CHUNK, nt(r.cot[...], r.wd[j]))

    def back(j):
        arrived(main, j)
        grads = main.grads[j].reshape(256, 2 * CHUNK)
        for n in range(2):
            at = pl.ds(n * 512, 512)
            r.acc[:, at] += nt(grads, r.wgu[j, at, :])

    for load in small_loads()[:2]:
        load.wait()
    pl.semaphore_wait(barrier, len(partners))
    pair_cot().start()

    def tick(t, carry):
        def stage(lag, run):
            @pl.when((t >= lag) & (t < nj + lag))
            def _():
                run(t - lag)

        def once(at, run):
            pl.when(t == at)(run)

        def matmul_stage(j):
            matmuls(j)
            to_sib(main, j).start()

        def special_matmul_stage():
            special_matmuls()
            to_sib(special, 0).start()

        def grad_stage(j):
            totals(main, j)
            spread(main, j)

        stage(0, matmul_stage)
        once(0, special_matmul_stage)
        stage(LAG_ADD, lambda j: add(main, j))
        once(LAG_ADD, lambda: add(special, 0))
        stage(LAG_RELAY, lambda j: relay(main, j))
        once(LAG_RELAY, lambda: relay(special, 0))
        stage(LAG_GRAD, grad_stage)
        once(LAG_GRAD, special_totals)
        once(LAG_GRAD + 1, special_spread)
        stage(LAG_FORWARD, lambda j: forward(main, j))
        once(LAG_FORWARD + 1, lambda: forward(special, 0))
        stage(LAG_LAST, lambda j: last(main, j))
        once(LAG_LAST + 1, lambda: last(special, 0))
        once(LAG_BACK, special_back)
        stage(LAG_BACK, back)
        once(LAG_BACK + 4, special_pair)
        return carry

    lax.fori_loop(0, nj + LAG_BACK, tick, 0)

    for k in range(1, nh):
        rows = pl.ds(pl.multiple_of(lax.rem(h + k, nh) * 32, 32), 32)
        r.xs[k] = r.acc[rows, :].astype(BF16)
        x_copy(k).start()
    total = r.acc[pl.ds(pl.multiple_of(h * 32, 32), 32), :] + r.xcode[...]
    for k in range(1, nh):
        x_copy(k).wait_recv()
        total += r.xr[k].astype(F32)
    r.o_x[...] = total.astype(BF16)

    def sent(j, carry):
        all_sent(main, j)
        return carry

    lax.fori_loop(0, nj, sent, 0)
    all_sent(special, 0)
    for copy in (pair_cot(), pair_routes(), pair_codes(), pair_shared()):
        copy.wait_send()
    for k in range(1, nh):
        code_copy(k).wait_send()
        x_copy(k).wait_send()


def solution(mesh):
    nh = mesh.shape["head"]

    def step(tokens, cotangent, w_gate, w_up, w_down, factor, heads, routes):
        rows, width = tokens.shape
        nj = w_gate.shape[1] // CHUNK
        rank, count = factor.shape[1], heads.shape[0]
        shapes = {}

        def vmem(name, shape, dtype=BF16):
            shapes[name] = pltpu.VMEM(shape, dtype)

        vmem("tok", (rows, width))
        vmem("cot", (rows, width))
        vmem("p_cot", (rows, width))
        vmem("rts", (rows, 1), jnp.int32)
        vmem("hup", (count, rank, width))
        vmem("cdf", (width, rank))
        vmem("cdf2", (width, 2 * rank))
        vmem("wgu", (nj, width, 2 * CHUNK))
        vmem("wd", (nj, CHUNK, width))
        vmem("t_wg", (width, TAIL))
        vmem("t_wu", (width, TAIL))
        vmem("t_wd", (TAIL, width))
        vmem("raw_g", (width, w_gate.shape[1] - nj * CHUNK))
        vmem("raw_u", (width, w_gate.shape[1] - nj * CHUNK))
        for kind, n, unit, extra in (("m", nj, CHUNK, 0), ("t", 1, TAIL, TAIL)):
            full = 3 * unit + extra
            vmem(kind + "_part", (n, 2, 4, 32, full))
            vmem(kind + "_sibs", (n, 4, 32, full))
            for name in ("s1", "s2", "s3", "r1", "r2", "r3"):
                vmem(kind + "_" + name, (n, 32, full))
            vmem(kind + "_grads", (n, 8, 32, 2 * unit + extra))
            shapes[kind + "_send"] = pltpu.SemaphoreType.DMA((n, 11))
            shapes[kind + "_recv"] = pltpu.SemaphoreType.DMA((n, 11))
        vmem("rb", (rows, 2 * rank))
        vmem("p_rb", (rows, 2 * rank))
        vmem("codes", (rows, 2 * rank))
        vmem("p_codes", (rows, 2 * rank))
        vmem("shared", (width, rank))
        vmem("p_shared", (width, rank))
        vmem("mine", (32, 2 * rank))
        vmem("hx", (nh, 32, 2 * rank))
        vmem("xs", (nh, 32, width))
        vmem("xr", (nh, 32, width))
        vmem("acc", (rows, width), F32)
        vmem("xcode", (32, width), F32)
        vmem("uph", (count, rank, width), F32)
        shapes["o_send"] = pltpu.SemaphoreType.DMA((4 + 2 * nh,))
        shapes["o_recv"] = pltpu.SemaphoreType.DMA((4 + 2 * nh,))
        shapes["small_sem"] = pltpu.SemaphoreType.DMA((8,))
        shapes["load_sem"] = pltpu.SemaphoreType.DMA((nj, 3))
        names = ["tokens", "cotangent", "w_gate", "w_up", "w_down", "factor", "heads", "routes"]
        names += ["o_x", "o_shared", "o_heads"] + list(shapes)

        def kernel(*refs):
            body(names, nj, nh, *refs)

        any_space = pl.BlockSpec(memory_space=pl.ANY)
        return pl.pallas_call(
            kernel,
            out_shape=(
                jax.ShapeDtypeStruct((32, width), BF16),
                jax.ShapeDtypeStruct((width, rank), F32),
                jax.ShapeDtypeStruct((count, rank, width), F32),
            ),
            in_specs=[any_space] * 8,
            out_specs=(pl.BlockSpec(memory_space=pltpu.VMEM),) * 3,
            scratch_shapes=list(shapes.values()),
            compiler_params=pltpu.CompilerParams(
                collective_id=0, has_side_effects=True, vmem_limit_bytes=60 * 1024 * 1024
            ),
            name="ffn_backward",
        )(tokens, cotangent, w_gate, w_up, w_down, factor, heads, routes)

    placed = (
        P("dp", "tensor"),
        P("dp", "tensor"),
        P("tensor", "head"),
        P("tensor", "head"),
        P("head", "tensor"),
        P("tensor", None),
        P("head", None, "tensor"),
        P("dp", None),
    )
    return jax.shard_map(
        step,
        mesh=mesh,
        in_specs=placed,
        out_specs=(P(("dp", "head"), "tensor"), P("tensor", None), P("head", None, "tensor")),
        check_vma=False,
    )
```

```python
import jax
import jax.numpy as jnp
from jax import lax
from jax.experimental import pallas as pl
from jax.experimental.pallas import tpu as pltpu
from jax.sharding import PartitionSpec as P

ADAPTER_SCALE = 2.0
MESH = pl.DeviceIdType.MESH
F32, BF16 = jnp.float32, jnp.bfloat16
CHUNK = 512
TAIL = 128
LAG_ADD, LAG_RELAY, LAG_GRAD, LAG_FORWARD, LAG_LAST, LAG_BACK = 1, 2, 3, 4, 5, 6


class Box:
    pass


def nt(left, right):
    return lax.dot_general(left, right, (((1,), (1,)), ((), ())), preferred_element_type=F32)


def tn(left, right):
    return lax.dot_general(left, right, (((0,), (0,)), ((), ())), preferred_element_type=F32)


def body(names, nj, nh, *refs):
    r = Box()
    for name, ref in zip(names, refs):
        setattr(r, name, ref)
    hidden = nj * CHUNK
    tail = r.w_gate.shape[0] - hidden
    tau, h, dp = lax.axis_index("tensor"), lax.axis_index("head"), lax.axis_index("dp")
    x, c = tau // 2, lax.rem(tau, 2)
    step = 2 * c - 1
    xp, xm, x2 = lax.rem(x + step + 4, 4), lax.rem(x - step + 4, 4), lax.rem(x + 2, 4)
    sib = {"tensor": 2 * x + 1 - c}
    nxt, prv = {"tensor": 2 * xp + c}, {"tensor": 2 * xm + c}
    pair = {"dp": 1 - dp}

    def head_peer(k):
        return {"head": lax.rem(h + k, nh)}

    barrier = pltpu.get_barrier_semaphore()
    partners = [sib, nxt, prv, pair] + [head_peer(k) for k in range(1, nh)]
    for partner in partners:
        pl.semaphore_signal(barrier, inc=1, device_id=partner, device_id_type=MESH)

    def local(src, dst, sem):
        return pltpu.make_async_copy(src, dst, sem)

    def small_loads():
        return [
            local(r.tokens, r.tok, r.small_sem.at[0]),
            local(r.cotangent, r.cot, r.small_sem.at[1]),
            local(r.routes, r.rts, r.small_sem.at[2]),
            local(r.heads, r.hup, r.small_sem.at[3]),
            local(r.factor, r.cdf, r.small_sem.at[4]),
        ]

    def chunk_loads(j):
        rows = pl.ds(pl.multiple_of(j * CHUNK, CHUNK), CHUNK)
        return [
            local(r.w_gate.at[rows, :], r.wgu.at[j, pl.ds(0, CHUNK), :], r.load_sem.at[j, 0]),
            local(r.w_up.at[rows, :], r.wgu.at[j, pl.ds(CHUNK, CHUNK), :], r.load_sem.at[j, 1]),
            local(r.w_down.at[rows, :], r.wd.at[j], r.load_sem.at[j, 2]),
        ]

    def tail_loads():
        rows = pl.ds(hidden, tail)
        return [
            local(r.w_gate.at[rows, :], r.t_wgu.at[pl.ds(0, tail), :], r.small_sem.at[5]),
            local(r.w_up.at[rows, :], r.t_wgu.at[pl.ds(TAIL, tail), :], r.small_sem.at[6]),
            local(r.w_down.at[rows, :], r.t_wd.at[pl.ds(0, tail), :], r.small_sem.at[7]),
        ]

    first = small_loads()
    first[0].start()
    for load in chunk_loads(0):
        load.start()
    for load in first[1:]:
        load.start()
    r.t_wgu[...] = jnp.zeros_like(r.t_wgu)
    r.t_wd[...] = jnp.zeros_like(r.t_wd)
    for load in tail_loads():
        load.start()

    def start_chunk(j, carry):
        for load in chunk_loads(j):
            load.start()
        return carry

    lax.fori_loop(1, nj, start_chunk, 0)

    def main():
        b = Box()
        b.part, b.sibs = r.m_part, r.m_sibs
        b.s1, b.s2, b.s3, b.r1, b.r2, b.r3 = r.m_s1, r.m_s2, r.m_s3, r.m_r1, r.m_r2, r.m_r3
        b.grads, b.send, b.recv, b.width = r.m_grads, r.m_send, r.m_recv, CHUNK
        return b

    def special():
        b = Box()
        b.part, b.sibs = r.t_part, r.t_sibs
        b.s1, b.s2, b.s3, b.r1, b.r2, b.r3 = r.t_s1, r.t_s2, r.t_s3, r.t_r1, r.t_r2, r.t_r3
        b.grads, b.send, b.recv, b.width = r.t_grads, r.t_send, r.t_recv, TAIL
        return b

    main, special = main(), special()

    def remote(b, j, i, src, dst, to):
        return pltpu.make_async_remote_copy(
            src_ref=src,
            dst_ref=dst,
            send_sem=b.send.at[j, i],
            recv_sem=b.recv.at[j, i],
            device_id=to,
            device_id_type=MESH,
        )

    def to_sib(b, j):
        return remote(b, j, 0, b.part.at[j, 1 - c], b.sibs.at[j], sib)

    def sum_far(b, j):
        return remote(b, j, 1, b.s1.at[j], b.r1.at[j], nxt)

    def sum_near(b, j):
        return remote(b, j, 2, b.s2.at[j], b.r2.at[j], prv)

    def sum_on(b, j):
        return remote(b, j, 3, b.s3.at[j], b.r3.at[j], nxt)

    def grad(b, j, i, slot, to):
        return remote(b, j, i, b.grads.at[j, slot], b.grads.at[j, slot], to)

    own, far, near, ahead = 2 * x + c, 2 * x2 + c, 2 * xm + c, 2 * xp + c
    sib_own, sib_far, sib_near, sib_ahead = (
        2 * x + 1 - c,
        2 * x2 + 1 - c,
        2 * xm + 1 - c,
        2 * xp + 1 - c,
    )

    def add(b, j):
        to_sib(b, j).wait_recv()
        b.s1[j] = (b.part[j, c, x2].astype(F32) + b.sibs[j, x2].astype(F32)).astype(BF16)
        sum_far(b, j).start()
        b.s2[j] = (b.part[j, c, xm].astype(F32) + b.sibs[j, xm].astype(F32)).astype(BF16)
        sum_near(b, j).start()

    def relay(b, j):
        sum_far(b, j).wait_recv()
        b.s3[j] = (
            b.r1[j].astype(F32) + b.part[j, c, xp].astype(F32) + b.sibs[j, xp].astype(F32)
        ).astype(BF16)
        sum_on(b, j).start()

    def totals(b, j):
        sum_near(b, j).wait_recv()
        sum_on(b, j).wait_recv()
        width = b.width

        def part(lo, size):
            at = pl.ds(lo, size)
            return (
                b.r3[j, :, at].astype(F32)
                + b.r2[j, :, at].astype(F32)
                + b.part[j, c, x, :, at].astype(F32)
                + b.sibs[j, x, :, at].astype(F32)
            )

        gate, up, back = (part(i * width, width) for i in range(3))
        sig = jax.nn.sigmoid(gate)
        b.grads[j, own, :, pl.ds(0, width)] = (
            back * up * sig * (1.0 + gate * (1.0 - sig))
        ).astype(BF16)
        b.grads[j, own, :, pl.ds(width, width)] = (back * gate * sig).astype(BF16)
        return part

    def spread(b, j):
        grad(b, j, 4, own, nxt).start()
        grad(b, j, 5, own, prv).start()
        grad(b, j, 6, own, sib).start()

    def forward(b, j):
        grad(b, j, 4, near, nxt).wait_recv()
        grad(b, j, 7, near, nxt).start()
        grad(b, j, 8, near, sib).start()
        grad(b, j, 5, ahead, prv).wait_recv()
        grad(b, j, 9, ahead, sib).start()

    def last(b, j):
        grad(b, j, 7, far, nxt).wait_recv()
        grad(b, j, 10, far, sib).start()

    def arrived(b, j):
        grad(b, j, 6, sib_own, sib).wait_recv()
        grad(b, j, 8, sib_ahead, sib).wait_recv()
        grad(b, j, 9, sib_near, sib).wait_recv()
        grad(b, j, 10, sib_far, sib).wait_recv()

    def all_sent(b, j):
        for copy in (to_sib(b, j), sum_far(b, j), sum_near(b, j), sum_on(b, j)):
            copy.wait_send()
        grad(b, j, 4, own, nxt).wait_send()
        grad(b, j, 5, own, prv).wait_send()
        grad(b, j, 6, own, sib).wait_send()
        grad(b, j, 7, near, nxt).wait_send()
        grad(b, j, 8, near, sib).wait_send()
        grad(b, j, 9, ahead, sib).wait_send()
        grad(b, j, 10, far, sib).wait_send()

    def store_part(b, j, lo, value):
        for q in range(4):
            for core in range(2):
                at = (2 * q + core) * 32
                b.part[j, core, q, :, pl.ds(lo, value.shape[1])] = value[at : at + 32].astype(BF16)

    def other(i, src, dst, to):
        return pltpu.make_async_remote_copy(
            src_ref=src,
            dst_ref=dst,
            send_sem=r.o_send.at[i],
            recv_sem=r.o_recv.at[i],
            device_id=to,
            device_id_type=MESH,
        )

    def pair_cot():
        return other(0, r.cot, r.p_cot, pair)

    def pair_routes():
        return other(1, r.rb, r.p_rb, pair)

    def pair_codes():
        return other(2, r.codes, r.p_codes, pair)

    def pair_shared():
        return other(3, r.shared, r.p_shared, pair)

    def code_copy(k):
        return other(4 + k, r.mine, r.hx.at[k], head_peer(k))

    def x_copy(k):
        return other(4 + nh + k, r.xs.at[k], r.xr.at[k], head_peer(k))

    first_head = h * r.hup.shape[0]
    rank = r.cdf.shape[0]

    def lanes(shape):
        return lax.broadcasted_iota(jnp.int32, shape, 1)

    def special_matmuls():
        for load in small_loads()[2:] + tail_loads():
            load.wait()
        factor = r.cdf[...]
        upper = jnp.concatenate([jnp.zeros_like(factor), factor], axis=0)
        tok, cot = r.tok[...], r.cot[...]
        store_part(special, 0, 0, nt(tok, r.t_wgu[...]))
        store_part(special, 0, 2 * TAIL, nt(cot, r.t_wd[...]))
        codes = nt(tok, upper)
        row = r.rts[...].astype(F32)
        routes = jnp.broadcast_to(row, (2 * rank, row.shape[1])).T
        r.rb[...] = routes.astype(BF16)
        pair_routes().start()
        total = jnp.zeros_like(codes)
        half = (lanes(codes.shape) >= rank).astype(F32)
        base = first_head.astype(F32) + half
        for p in range(r.hup.shape[0] // 2):
            flat = jnp.concatenate([r.hup[2 * p], r.hup[2 * p + 1]], axis=0)
            total += jnp.where(routes == base + 2.0 * p, nt(cot, flat), 0.0)
        total = ADAPTER_SCALE * (total + pltpu.roll(total, rank, 1))
        store_part(special, 0, 3 * TAIL, jnp.where(half == 0.0, total, codes))

    def special_totals():
        part = totals(special, 0)
        r.mine[...] = part(3 * TAIL, TAIL).astype(BF16)
        for k in range(1, nh):
            code_copy(k).start()

    def special_spread():
        mine = r.mine[...].astype(F32)
        total = mine
        for k in range(1, nh):
            code_copy(k).wait_recv()
            total += r.hx[k].astype(F32)
        total = jnp.where(lanes(mine.shape) < rank, total, mine)
        special.grads[0, own, :, pl.ds(2 * TAIL, TAIL)] = total.astype(BF16)
        spread(special, 0)

    def heads_out(p):
        at = pl.ds(2 * p, 2)
        return local(r.uph.at[at], r.o_heads.at[at], r.out_sem.at[p])

    def up_heads(codes, routes, cot, fresh):
        both = jnp.where(
            lanes(codes.shape) < rank, pltpu.roll(codes.astype(F32), rank, 1), codes.astype(F32)
        )
        half = (lanes(codes.shape) >= rank).astype(F32)
        base = first_head.astype(F32) + half
        for p in range(r.hup.shape[0] // 2):
            chosen = jnp.where(routes.astype(F32) == base + 2.0 * p, both, 0.0).astype(BF16)
            grads = (ADAPTER_SCALE * tn(chosen, cot)).reshape(2, rank, cot.shape[1])
            if fresh:
                r.uph[pl.ds(2 * p, 2)] = grads
            else:
                r.uph[pl.ds(2 * p, 2)] += grads
                heads_out(p).start()

    def special_back():
        arrived(special, 0)
        grads = special.grads[0, :, :, pl.ds(0, 2 * TAIL)].reshape(256, 2 * TAIL)
        r.acc[...] = jnp.dot(grads, r.t_wgu[...], preferred_element_type=F32)
        codes = special.grads[0, :, :, pl.ds(2 * TAIL, TAIL)].reshape(256, TAIL)
        r.codes[...] = codes
        pair_codes().start()
        r.shared[...] = tn(codes, r.tok[...])[:rank].astype(BF16)
        pair_shared().start()
        up_heads(codes, r.rb[...], r.cot[...], True)
        mine = special.grads[0, h, :, pl.ds(2 * TAIL, TAIL)]
        factor = r.cdf[...]
        lower = jnp.concatenate([factor, jnp.zeros_like(factor)], axis=0)
        r.xcode[...] = jnp.dot(mine, lower, preferred_element_type=F32)

    def special_pair():
        pair_cot().wait_recv()
        pair_routes().wait_recv()
        pair_codes().wait_recv()
        up_heads(r.p_codes[...], r.p_rb[...], r.p_cot[...], False)
        pair_shared().wait_recv()
        r.o_shared[...] = r.shared[...].astype(F32) + r.p_shared[...].astype(F32)

    def matmuls(j):
        loads = chunk_loads(j)
        loads[0].wait()
        tok = r.tok[...]
        store_part(main, j, 0, nt(tok, r.wgu[j, pl.ds(0, CHUNK), :]))
        loads[1].wait()
        store_part(main, j, CHUNK, nt(tok, r.wgu[j, pl.ds(CHUNK, CHUNK), :]))
        loads[2].wait()
        store_part(main, j, 2 * CHUNK, nt(r.cot[...], r.wd[j]))

    def back(j):
        arrived(main, j)
        grads = main.grads[j].reshape(256, 2 * CHUNK)
        for n in range(2):
            at = pl.ds(n * 512, 512)
            r.acc[:, at] += jnp.dot(grads, r.wgu[j, :, at], preferred_element_type=F32)

    for load in small_loads()[:2]:
        load.wait()
    pl.semaphore_wait(barrier, len(partners))
    pair_cot().start()

    def tick(t, carry):
        def stage(lag, run):
            @pl.when((t >= lag) & (t < nj + lag))
            def _():
                run(t - lag)

        def once(at, run):
            pl.when(t == at)(run)

        def matmul_stage(j):
            matmuls(j)
            to_sib(main, j).start()

        def special_matmul_stage():
            special_matmuls()
            to_sib(special, 0).start()

        def grad_stage(j):
            totals(main, j)
            spread(main, j)

        stage(0, matmul_stage)
        once(0, special_matmul_stage)
        stage(LAG_ADD, lambda j: add(main, j))
        once(LAG_ADD, lambda: add(special, 0))
        stage(LAG_RELAY, lambda j: relay(main, j))
        once(LAG_RELAY, lambda: relay(special, 0))
        stage(LAG_GRAD, grad_stage)
        once(LAG_GRAD, special_totals)
        once(LAG_GRAD + 1, special_spread)
        stage(LAG_FORWARD, lambda j: forward(main, j))
        once(LAG_FORWARD + 1, lambda: forward(special, 0))
        stage(LAG_LAST, lambda j: last(main, j))
        once(LAG_LAST + 1, lambda: last(special, 0))
        once(LAG_BACK, special_back)
        stage(LAG_BACK, back)
        once(LAG_BACK + 4, special_pair)
        return carry

    lax.fori_loop(0, nj + LAG_BACK, tick, 0)

    for k in range(1, nh):
        rows = pl.ds(pl.multiple_of(lax.rem(h + k, nh) * 32, 32), 32)
        r.xs[k] = r.acc[rows, :].astype(BF16)
        x_copy(k).start()
    total = r.acc[pl.ds(pl.multiple_of(h * 32, 32), 32), :] + r.xcode[...]
    for k in range(1, nh):
        x_copy(k).wait_recv()
        total += r.xr[k].astype(F32)
    r.o_x[...] = total.astype(BF16)

    def sent(j, carry):
        all_sent(main, j)
        return carry

    lax.fori_loop(0, nj, sent, 0)
    all_sent(special, 0)
    for p in range(r.hup.shape[0] // 2):
        heads_out(p).wait()
    for copy in (pair_cot(), pair_routes(), pair_codes(), pair_shared()):
        copy.wait_send()
    for k in range(1, nh):
        code_copy(k).wait_send()
        x_copy(k).wait_send()


def finish(x_in, shared_in, heads_in, x_out, shared_out, heads_out, sems):
    count = heads_in.shape[0]
    copies = [
        pltpu.make_async_copy(heads_in.at[e], heads_out.at[e], sems.at[e]) for e in range(count)
    ]
    copies.append(pltpu.make_async_copy(x_in, x_out, sems.at[count]))
    copies.append(pltpu.make_async_copy(shared_in, shared_out, sems.at[count + 1]))
    for copy in copies:
        copy.start()
    for copy in copies:
        copy.wait()


def solution(mesh):
    nh = mesh.shape["head"]

    def step(tokens, cotangent, w_gate, w_up, w_down, factor, heads, routes):
        rows, width = tokens.shape
        w_gate, w_up, factor, routes = w_gate.T, w_up.T, factor.T, routes.T
        nj = w_gate.shape[0] // CHUNK
        rank, count = factor.shape[0], heads.shape[0]
        shapes = {}

        def vmem(name, shape, dtype=BF16):
            shapes[name] = pltpu.VMEM(shape, dtype)

        vmem("tok", (rows, width))
        vmem("cot", (rows, width))
        vmem("p_cot", (rows, width))
        vmem("rts", (1, rows), jnp.int32)
        vmem("hup", (count, rank, width))
        vmem("cdf", (rank, width))
        vmem("wgu", (nj, 2 * CHUNK, width))
        vmem("wd", (nj, CHUNK, width))
        vmem("t_wgu", (2 * TAIL, width))
        vmem("t_wd", (TAIL, width))
        for kind, n, unit, extra in (("m", nj, CHUNK, 0), ("t", 1, TAIL, TAIL)):
            full = 3 * unit + extra
            vmem(kind + "_part", (n, 2, 4, 32, full))
            vmem(kind + "_sibs", (n, 4, 32, full))
            for name in ("s1", "s2", "s3", "r1", "r2", "r3"):
                vmem(kind + "_" + name, (n, 32, full))
            vmem(kind + "_grads", (n, 8, 32, 2 * unit + extra))
            shapes[kind + "_send"] = pltpu.SemaphoreType.DMA((n, 11))
            shapes[kind + "_recv"] = pltpu.SemaphoreType.DMA((n, 11))
        vmem("rb", (rows, 2 * rank))
        vmem("p_rb", (rows, 2 * rank))
        vmem("codes", (rows, 2 * rank))
        vmem("p_codes", (rows, 2 * rank))
        vmem("shared", (rank, width))
        vmem("p_shared", (rank, width))
        vmem("mine", (32, 2 * rank))
        vmem("hx", (nh, 32, 2 * rank))
        vmem("xs", (nh, 32, width))
        vmem("xr", (nh, 32, width))
        vmem("acc", (rows, width), F32)
        vmem("xcode", (32, width), F32)
        vmem("uph", (count, rank, width), F32)
        shapes["o_send"] = pltpu.SemaphoreType.DMA((4 + 2 * nh,))
        shapes["o_recv"] = pltpu.SemaphoreType.DMA((4 + 2 * nh,))
        shapes["out_sem"] = pltpu.SemaphoreType.DMA((count // 2,))
        shapes["small_sem"] = pltpu.SemaphoreType.DMA((8,))
        shapes["load_sem"] = pltpu.SemaphoreType.DMA((nj, 3))
        names = ["tokens", "cotangent", "w_gate", "w_up", "w_down", "factor", "heads", "routes"]
        names += ["o_x", "o_shared", "o_heads"] + list(shapes)

        def kernel(*refs):
            body(names, nj, nh, *refs)

        any_space = pl.BlockSpec(memory_space=pl.ANY)
        made = pl.pallas_call(
            kernel,
            out_shape=(
                jax.ShapeDtypeStruct((32, width), BF16),
                jax.ShapeDtypeStruct((rank, width), F32),
                jax.ShapeDtypeStruct((count, rank, width), F32),
            ),
            in_specs=[any_space] * 8,
            out_specs=(
                pl.BlockSpec(memory_space=pltpu.VMEM),
                pl.BlockSpec(memory_space=pltpu.VMEM),
                any_space,
            ),
            scratch_shapes=list(shapes.values()),
            compiler_params=pltpu.CompilerParams(
                collective_id=0, has_side_effects=True, vmem_limit_bytes=60 * 1024 * 1024
            ),
            name="ffn_backward",
        )(tokens, cotangent, w_gate, w_up, w_down, factor, heads, routes)
        grad_x, shared, up = pl.pallas_call(
            finish,
            out_shape=tuple(jax.ShapeDtypeStruct(m.shape, m.dtype) for m in made),
            in_specs=[any_space] * 3,
            out_specs=(any_space,) * 3,
            scratch_shapes=[pltpu.SemaphoreType.DMA((count + 2,))],
            name="write_out",
        )(*made)
        return grad_x, shared.T, up

    placed = (
        P("dp", "tensor"),
        P("dp", "tensor"),
        P("tensor", "head"),
        P("tensor", "head"),
        P("head", "tensor"),
        P("tensor", None),
        P("head", None, "tensor"),
        P("dp", None),
    )
    return jax.shard_map(
        step,
        mesh=mesh,
        in_specs=placed,
        out_specs=(P(("dp", "head"), "tensor"), P("tensor", None), P("head", None, "tensor")),
        check_vma=False,
    )
```

```python
import jax
import jax.numpy as jnp
from jax import lax
from jax.experimental import pallas as pl
from jax.experimental.pallas import tpu as pltpu
from jax.sharding import PartitionSpec as P

ADAPTER_SCALE = 2.0
MESH = pl.DeviceIdType.MESH
F32, BF16 = jnp.float32, jnp.bfloat16
CHUNK = 512
TAIL = 128
LAG_ADD, LAG_RELAY, LAG_GRAD, LAG_FORWARD, LAG_LAST, LAG_BACK = 1, 3, 5, 7, 9, 11


class Box:
    pass


def nt(left, right):
    return lax.dot_general(left, right, (((1,), (1,)), ((), ())), preferred_element_type=F32)


def tn(left, right):
    return lax.dot_general(left, right, (((0,), (0,)), ((), ())), preferred_element_type=F32)


def body(names, nj, nh, *refs):
    r = Box()
    for name, ref in zip(names, refs):
        setattr(r, name, ref)
    hidden = nj * CHUNK
    tail = r.w_gate.shape[0] - hidden
    tau, h, dp = lax.axis_index("tensor"), lax.axis_index("head"), lax.axis_index("dp")
    x, c = tau // 2, lax.rem(tau, 2)
    step = 2 * c - 1
    xp, xm, x2 = lax.rem(x + step + 4, 4), lax.rem(x - step + 4, 4), lax.rem(x + 2, 4)
    sib = {"tensor": 2 * x + 1 - c}
    nxt, prv = {"tensor": 2 * xp + c}, {"tensor": 2 * xm + c}
    pair = {"dp": 1 - dp}

    def head_peer(k):
        return {"head": lax.rem(h + k, nh)}

    barrier = pltpu.get_barrier_semaphore()
    partners = [sib, nxt, prv, pair] + [head_peer(k) for k in range(1, nh)]
    for partner in partners:
        pl.semaphore_signal(barrier, inc=1, device_id=partner, device_id_type=MESH)

    def local(src, dst, sem):
        return pltpu.make_async_copy(src, dst, sem)

    def small_loads():
        return [
            local(r.tokens, r.tok, r.small_sem.at[0]),
            local(r.cotangent, r.cot, r.small_sem.at[1]),
            local(r.routes, r.rts, r.small_sem.at[2]),
            local(r.heads, r.hup, r.small_sem.at[3]),
            local(r.factor, r.cdf, r.small_sem.at[4]),
        ]

    def chunk_loads(j):
        rows = pl.ds(pl.multiple_of(j * CHUNK, CHUNK), CHUNK)
        return [
            local(r.w_gate.at[rows, :], r.wgu.at[j, pl.ds(0, CHUNK), :], r.load_sem.at[j, 0]),
            local(r.w_up.at[rows, :], r.wgu.at[j, pl.ds(CHUNK, CHUNK), :], r.load_sem.at[j, 1]),
            local(r.w_down.at[rows, :], r.wd.at[j], r.load_sem.at[j, 2]),
        ]

    def tail_loads():
        rows = pl.ds(hidden, tail)
        return [
            local(r.w_gate.at[rows, :], r.t_wgu.at[pl.ds(0, tail), :], r.small_sem.at[5]),
            local(r.w_up.at[rows, :], r.t_wgu.at[pl.ds(TAIL, tail), :], r.small_sem.at[6]),
            local(r.w_down.at[rows, :], r.t_wd.at[pl.ds(0, tail), :], r.small_sem.at[7]),
        ]

    first = small_loads()
    first[0].start()
    for load in chunk_loads(0):
        load.start()
    for load in first[1:]:
        load.start()
    r.t_wgu[...] = jnp.zeros_like(r.t_wgu)
    r.t_wd[...] = jnp.zeros_like(r.t_wd)
    for load in tail_loads():
        load.start()

    def start_chunk(j, carry):
        for load in chunk_loads(j):
            load.start()
        return carry

    lax.fori_loop(1, nj, start_chunk, 0)

    def main():
        b = Box()
        b.part, b.sibs = r.m_part, r.m_sibs
        b.s1, b.s2, b.s3, b.r1, b.r2, b.r3 = r.m_s1, r.m_s2, r.m_s3, r.m_r1, r.m_r2, r.m_r3
        b.grads, b.send, b.recv, b.width = r.m_grads, r.m_send, r.m_recv, CHUNK
        return b

    def special():
        b = Box()
        b.part, b.sibs = r.t_part, r.t_sibs
        b.s1, b.s2, b.s3, b.r1, b.r2, b.r3 = r.t_s1, r.t_s2, r.t_s3, r.t_r1, r.t_r2, r.t_r3
        b.grads, b.send, b.recv, b.width = r.t_grads, r.t_send, r.t_recv, TAIL
        return b

    main, special = main(), special()

    def remote(b, j, i, src, dst, to):
        return pltpu.make_async_remote_copy(
            src_ref=src,
            dst_ref=dst,
            send_sem=b.send.at[j, i],
            recv_sem=b.recv.at[j, i],
            device_id=to,
            device_id_type=MESH,
        )

    def to_sib(b, j):
        return remote(b, j, 0, b.part.at[j, 1 - c], b.sibs.at[j], sib)

    def sum_far(b, j):
        return remote(b, j, 1, b.s1.at[j], b.r1.at[j], nxt)

    def sum_near(b, j):
        return remote(b, j, 2, b.s2.at[j], b.r2.at[j], prv)

    def sum_on(b, j):
        return remote(b, j, 3, b.s3.at[j], b.r3.at[j], nxt)

    def grad(b, j, i, slot, to):
        return remote(b, j, i, b.grads.at[j, slot], b.grads.at[j, slot], to)

    own, far, near, ahead = 2 * x + c, 2 * x2 + c, 2 * xm + c, 2 * xp + c
    sib_own, sib_far, sib_near, sib_ahead = (
        2 * x + 1 - c,
        2 * x2 + 1 - c,
        2 * xm + 1 - c,
        2 * xp + 1 - c,
    )

    def add(b, j):
        to_sib(b, j).wait_recv()
        b.s1[j] = (b.part[j, c, x2].astype(F32) + b.sibs[j, x2].astype(F32)).astype(BF16)
        sum_far(b, j).start()
        b.s2[j] = (b.part[j, c, xm].astype(F32) + b.sibs[j, xm].astype(F32)).astype(BF16)
        sum_near(b, j).start()

    def relay(b, j):
        sum_far(b, j).wait_recv()
        b.s3[j] = (
            b.r1[j].astype(F32) + b.part[j, c, xp].astype(F32) + b.sibs[j, xp].astype(F32)
        ).astype(BF16)
        sum_on(b, j).start()

    def totals(b, j):
        sum_near(b, j).wait_recv()
        sum_on(b, j).wait_recv()
        width = b.width

        def part(lo, size):
            at = pl.ds(lo, size)
            return (
                b.r3[j, :, at].astype(F32)
                + b.r2[j, :, at].astype(F32)
                + b.part[j, c, x, :, at].astype(F32)
                + b.sibs[j, x, :, at].astype(F32)
            )

        gate, up, back = (part(i * width, width) for i in range(3))
        sig = jax.nn.sigmoid(gate)
        b.grads[j, own, :, pl.ds(0, width)] = (
            back * up * sig * (1.0 + gate * (1.0 - sig))
        ).astype(BF16)
        b.grads[j, own, :, pl.ds(width, width)] = (back * gate * sig).astype(BF16)
        return part

    def spread(b, j):
        grad(b, j, 4, own, nxt).start()
        grad(b, j, 5, own, prv).start()
        grad(b, j, 6, own, sib).start()

    def forward(b, j):
        grad(b, j, 4, near, nxt).wait_recv()
        grad(b, j, 7, near, nxt).start()
        grad(b, j, 8, near, sib).start()
        grad(b, j, 5, ahead, prv).wait_recv()
        grad(b, j, 9, ahead, sib).start()

    def last(b, j):
        grad(b, j, 7, far, nxt).wait_recv()
        grad(b, j, 10, far, sib).start()

    def arrived(b, j):
        grad(b, j, 6, sib_own, sib).wait_recv()
        grad(b, j, 8, sib_ahead, sib).wait_recv()
        grad(b, j, 9, sib_near, sib).wait_recv()
        grad(b, j, 10, sib_far, sib).wait_recv()

    def all_sent(b, j):
        for copy in (to_sib(b, j), sum_far(b, j), sum_near(b, j), sum_on(b, j)):
            copy.wait_send()
        grad(b, j, 4, own, nxt).wait_send()
        grad(b, j, 5, own, prv).wait_send()
        grad(b, j, 6, own, sib).wait_send()
        grad(b, j, 7, near, nxt).wait_send()
        grad(b, j, 8, near, sib).wait_send()
        grad(b, j, 9, ahead, sib).wait_send()
        grad(b, j, 10, far, sib).wait_send()

    def store_part(b, j, lo, value):
        for q in range(4):
            for core in range(2):
                at = (2 * q + core) * 32
                b.part[j, core, q, :, pl.ds(lo, value.shape[1])] = value[at : at + 32].astype(BF16)

    def other(i, src, dst, to):
        return pltpu.make_async_remote_copy(
            src_ref=src,
            dst_ref=dst,
            send_sem=r.o_send.at[i],
            recv_sem=r.o_recv.at[i],
            device_id=to,
            device_id_type=MESH,
        )

    def pair_cot():
        return other(0, r.cot, r.p_cot, pair)

    def pair_routes():
        return other(1, r.rb, r.p_rb, pair)

    def pair_codes():
        return other(2, r.codes, r.p_codes, pair)

    def pair_shared():
        return other(3, r.shared, r.p_shared, pair)

    def code_copy(k):
        return other(4 + k, r.mine, r.hx.at[k], head_peer(k))

    def x_copy(k):
        return other(4 + nh + k, r.xs.at[k], r.xr.at[k], head_peer(k))

    first_head = h * r.hup.shape[0]
    rank = r.cdf.shape[0]

    def lanes(shape):
        return lax.broadcasted_iota(jnp.int32, shape, 1)

    def special_matmuls():
        for load in small_loads()[2:] + tail_loads():
            load.wait()
        factor = r.cdf[...]
        upper = jnp.concatenate([jnp.zeros_like(factor), factor], axis=0)
        tok, cot = r.tok[...], r.cot[...]
        store_part(special, 0, 0, nt(tok, r.t_wgu[...]))
        store_part(special, 0, 2 * TAIL, nt(cot, r.t_wd[...]))
        codes = nt(tok, upper)
        row = r.rts[...].astype(F32)
        routes = jnp.broadcast_to(row, (2 * rank, row.shape[1])).T
        r.rb[...] = routes.astype(BF16)
        pair_routes().start()
        total = jnp.zeros_like(codes)
        half = (lanes(codes.shape) >= rank).astype(F32)
        base = first_head.astype(F32) + half
        for p in range(r.hup.shape[0] // 2):
            flat = jnp.concatenate([r.hup[2 * p], r.hup[2 * p + 1]], axis=0)
            total += jnp.where(routes == base + 2.0 * p, nt(cot, flat), 0.0)
        total = ADAPTER_SCALE * (total + pltpu.roll(total, rank, 1))
        store_part(special, 0, 3 * TAIL, jnp.where(half == 0.0, total, codes))

    def special_totals():
        part = totals(special, 0)
        r.mine[...] = part(3 * TAIL, TAIL).astype(BF16)
        for k in range(1, nh):
            code_copy(k).start()

    def special_spread():
        mine = r.mine[...].astype(F32)
        total = mine
        for k in range(1, nh):
            code_copy(k).wait_recv()
            total += r.hx[k].astype(F32)
        total = jnp.where(lanes(mine.shape) < rank, total, mine)
        special.grads[0, own, :, pl.ds(2 * TAIL, TAIL)] = total.astype(BF16)
        spread(special, 0)

    def heads_out(p):
        at = pl.ds(2 * p, 2)
        return local(r.uph.at[at], r.o_heads.at[at], r.out_sem.at[p])

    def up_heads(codes, routes, cot, fresh):
        both = jnp.where(
            lanes(codes.shape) < rank, pltpu.roll(codes.astype(F32), rank, 1), codes.astype(F32)
        )
        half = (lanes(codes.shape) >= rank).astype(F32)
        base = first_head.astype(F32) + half
        for p in range(r.hup.shape[0] // 2):
            chosen = jnp.where(routes.astype(F32) == base + 2.0 * p, both, 0.0).astype(BF16)
            grads = (ADAPTER_SCALE * tn(chosen, cot)).reshape(2, rank, cot.shape[1])
            if fresh:
                r.uph[pl.ds(2 * p, 2)] = grads
            else:
                r.uph[pl.ds(2 * p, 2)] += grads
                heads_out(p).start()

    def special_back():
        arrived(special, 0)
        grads = special.grads[0, :, :, pl.ds(0, 2 * TAIL)].reshape(256, 2 * TAIL)
        r.acc[...] = jnp.dot(grads, r.t_wgu[...], preferred_element_type=F32)
        codes = special.grads[0, :, :, pl.ds(2 * TAIL, TAIL)].reshape(256, TAIL)
        r.codes[...] = codes
        pair_codes().start()
        r.shared[...] = tn(codes, r.tok[...])[:rank].astype(BF16)
        pair_shared().start()
        up_heads(codes, r.rb[...], r.cot[...], True)
        mine = special.grads[0, h, :, pl.ds(2 * TAIL, TAIL)]
        factor = r.cdf[...]
        lower = jnp.concatenate([factor, jnp.zeros_like(factor)], axis=0)
        r.xcode[...] = jnp.dot(mine, lower, preferred_element_type=F32)

    def special_pair():
        pair_cot().wait_recv()
        pair_routes().wait_recv()
        pair_codes().wait_recv()
        up_heads(r.p_codes[...], r.p_rb[...], r.p_cot[...], False)
        pair_shared().wait_recv()
        r.o_shared[...] = r.shared[...].astype(F32) + r.p_shared[...].astype(F32)

    def matmuls(j):
        loads = chunk_loads(j)
        loads[0].wait()
        tok = r.tok[...]
        store_part(main, j, 0, nt(tok, r.wgu[j, pl.ds(0, CHUNK), :]))
        loads[1].wait()
        store_part(main, j, CHUNK, nt(tok, r.wgu[j, pl.ds(CHUNK, CHUNK), :]))
        loads[2].wait()
        store_part(main, j, 2 * CHUNK, nt(r.cot[...], r.wd[j]))

    def back(j):
        arrived(main, j)
        grads = main.grads[j].reshape(256, 2 * CHUNK)
        for n in range(2):
            at = pl.ds(n * 512, 512)
            r.acc[:, at] += jnp.dot(grads, r.wgu[j, :, at], preferred_element_type=F32)

    for load in small_loads()[:2]:
        load.wait()
    pl.semaphore_wait(barrier, len(partners))
    pair_cot().start()

    def tick(t, carry):
        def stage(lag, run):
            @pl.when((t >= lag) & (t < nj + lag))
            def _():
                run(t - lag)

        def once(at, run):
            pl.when(t == at)(run)

        def matmul_stage(j):
            matmuls(j)
            to_sib(main, j).start()

        def special_matmul_stage():
            special_matmuls()
            to_sib(special, 0).start()

        def grad_stage(j):
            totals(main, j)
            spread(main, j)

        stage(0, matmul_stage)
        once(0, special_matmul_stage)
        stage(LAG_ADD, lambda j: add(main, j))
        once(LAG_ADD, lambda: add(special, 0))
        stage(LAG_RELAY, lambda j: relay(main, j))
        once(LAG_RELAY, lambda: relay(special, 0))
        stage(LAG_GRAD, grad_stage)
        once(LAG_GRAD, special_totals)
        once(LAG_GRAD + 1, special_spread)
        stage(LAG_FORWARD, lambda j: forward(main, j))
        once(LAG_FORWARD + 1, lambda: forward(special, 0))
        stage(LAG_LAST, lambda j: last(main, j))
        once(LAG_LAST + 1, lambda: last(special, 0))
        once(LAG_BACK, special_back)
        stage(LAG_BACK, back)
        once(LAG_BACK + 4, special_pair)
        return carry

    lax.fori_loop(0, nj + LAG_BACK, tick, 0)

    for k in range(1, nh):
        rows = pl.ds(pl.multiple_of(lax.rem(h + k, nh) * 32, 32), 32)
        r.xs[k] = r.acc[rows, :].astype(BF16)
        x_copy(k).start()
    total = r.acc[pl.ds(pl.multiple_of(h * 32, 32), 32), :] + r.xcode[...]
    for k in range(1, nh):
        x_copy(k).wait_recv()
        total += r.xr[k].astype(F32)
    r.o_x[...] = total.astype(BF16)

    def sent(j, carry):
        all_sent(main, j)
        return carry

    lax.fori_loop(0, nj, sent, 0)
    all_sent(special, 0)
    for p in range(r.hup.shape[0] // 2):
        heads_out(p).wait()
    for copy in (pair_cot(), pair_routes(), pair_codes(), pair_shared()):
        copy.wait_send()
    for k in range(1, nh):
        code_copy(k).wait_send()
        x_copy(k).wait_send()


def finish(x_in, shared_in, heads_in, x_out, shared_out, heads_out, x, shared, heads, came, left):
    count = heads_in.shape[0]
    steps = [(heads_in.at[e], heads.at[e], heads_out.at[e]) for e in range(count)]
    steps += [(shared_in, shared, shared_out), (x_in, x, x_out)]
    reads = [pltpu.make_async_copy(a, b, came.at[i]) for i, (a, b, _) in enumerate(steps)]
    writes = [pltpu.make_async_copy(b, c, left.at[i]) for i, (_, b, c) in enumerate(steps)]
    for read in reads:
        read.start()
    for read, write in zip(reads, writes):
        read.wait()
        write.start()
    for write in writes:
        write.wait()


def solution(mesh):
    nh = mesh.shape["head"]

    def step(tokens, cotangent, w_gate, w_up, w_down, factor, heads, routes):
        rows, width = tokens.shape
        w_gate, w_up, factor, routes = w_gate.T, w_up.T, factor.T, routes.T
        nj = w_gate.shape[0] // CHUNK
        rank, count = factor.shape[0], heads.shape[0]
        shapes = {}

        def vmem(name, shape, dtype=BF16):
            shapes[name] = pltpu.VMEM(shape, dtype)

        vmem("tok", (rows, width))
        vmem("cot", (rows, width))
        vmem("p_cot", (rows, width))
        vmem("rts", (1, rows), jnp.int32)
        vmem("hup", (count, rank, width))
        vmem("cdf", (rank, width))
        vmem("wgu", (nj, 2 * CHUNK, width))
        vmem("wd", (nj, CHUNK, width))
        vmem("t_wgu", (2 * TAIL, width))
        vmem("t_wd", (TAIL, width))
        for kind, n, unit, extra in (("m", nj, CHUNK, 0), ("t", 1, TAIL, TAIL)):
            full = 3 * unit + extra
            vmem(kind + "_part", (n, 2, 4, 32, full))
            vmem(kind + "_sibs", (n, 4, 32, full))
            for name in ("s1", "s2", "s3", "r1", "r2", "r3"):
                vmem(kind + "_" + name, (n, 32, full))
            vmem(kind + "_grads", (n, 8, 32, 2 * unit + extra))
            shapes[kind + "_send"] = pltpu.SemaphoreType.DMA((n, 11))
            shapes[kind + "_recv"] = pltpu.SemaphoreType.DMA((n, 11))
        vmem("rb", (rows, 2 * rank))
        vmem("p_rb", (rows, 2 * rank))
        vmem("codes", (rows, 2 * rank))
        vmem("p_codes", (rows, 2 * rank))
        vmem("shared", (rank, width))
        vmem("p_shared", (rank, width))
        vmem("mine", (32, 2 * rank))
        vmem("hx", (nh, 32, 2 * rank))
        vmem("xs", (nh, 32, width))
        vmem("xr", (nh, 32, width))
        vmem("acc", (rows, width), F32)
        vmem("xcode", (32, width), F32)
        vmem("uph", (count, rank, width), F32)
        shapes["o_send"] = pltpu.SemaphoreType.DMA((4 + 2 * nh,))
        shapes["o_recv"] = pltpu.SemaphoreType.DMA((4 + 2 * nh,))
        shapes["out_sem"] = pltpu.SemaphoreType.DMA((count // 2,))
        shapes["small_sem"] = pltpu.SemaphoreType.DMA((8,))
        shapes["load_sem"] = pltpu.SemaphoreType.DMA((nj, 3))
        names = ["tokens", "cotangent", "w_gate", "w_up", "w_down", "factor", "heads", "routes"]
        names += ["o_x", "o_shared", "o_heads"] + list(shapes)

        def kernel(*refs):
            body(names, nj, nh, *refs)

        any_space = pl.BlockSpec(memory_space=pl.ANY)
        made = pl.pallas_call(
            kernel,
            out_shape=(
                jax.ShapeDtypeStruct((32, width), BF16),
                jax.ShapeDtypeStruct((rank, width), F32),
                jax.ShapeDtypeStruct((count, rank, width), F32),
            ),
            in_specs=[any_space] * 8,
            out_specs=(
                pl.BlockSpec(memory_space=pltpu.VMEM),
                pl.BlockSpec(memory_space=pltpu.VMEM),
                any_space,
            ),
            scratch_shapes=list(shapes.values()),
            compiler_params=pltpu.CompilerParams(
                collective_id=0, has_side_effects=True, vmem_limit_bytes=60 * 1024 * 1024
            ),
            name="ffn_backward",
        )(tokens, cotangent, w_gate, w_up, w_down, factor, heads, routes)
        grad_x, shared, up = pl.pallas_call(
            finish,
            out_shape=tuple(jax.ShapeDtypeStruct(m.shape, m.dtype) for m in made),
            in_specs=[any_space] * 3,
            out_specs=(any_space,) * 3,
            scratch_shapes=[pltpu.VMEM(m.shape, m.dtype) for m in made]
            + [pltpu.SemaphoreType.DMA((count + 2,))] * 2,
            name="write_out",
        )(*made)
        return grad_x, shared.T, up

    placed = (
        P("dp", "tensor"),
        P("dp", "tensor"),
        P("tensor", "head"),
        P("tensor", "head"),
        P("head", "tensor"),
        P("tensor", None),
        P("head", None, "tensor"),
        P("dp", None),
    )
    return jax.shard_map(
        step,
        mesh=mesh,
        in_specs=placed,
        out_specs=(P(("dp", "head"), "tensor"), P("tensor", None), P("head", None, "tensor")),
        check_vma=False,
    )
```

```python
import jax
import jax.numpy as jnp
from jax import lax
from jax.experimental import pallas as pl
from jax.experimental.pallas import tpu as pltpu
from jax.sharding import PartitionSpec as P

ADAPTER_SCALE = 2.0
MESH = pl.DeviceIdType.MESH
F32, BF16 = jnp.float32, jnp.bfloat16
CHUNK = 512
TAIL = 128
LAG_ADD, LAG_RELAY, LAG_GRAD, LAG_FORWARD, LAG_LAST, LAG_BACK = 1, 3, 5, 7, 9, 11


class Box:
    pass


def nt(left, right):
    return lax.dot_general(left, right, (((1,), (1,)), ((), ())), preferred_element_type=F32)


def tn(left, right):
    return lax.dot_general(left, right, (((0,), (0,)), ((), ())), preferred_element_type=F32)


def body(names, nj, nh, *refs):
    r = Box()
    for name, ref in zip(names, refs):
        setattr(r, name, ref)
    hidden = nj * CHUNK
    tail = r.w_gate.shape[0] - hidden
    tau, h, dp = lax.axis_index("tensor"), lax.axis_index("head"), lax.axis_index("dp")
    x, c = tau // 2, lax.rem(tau, 2)
    step = 2 * c - 1
    xp, xm, x2 = lax.rem(x + step + 4, 4), lax.rem(x - step + 4, 4), lax.rem(x + 2, 4)
    sib = {"tensor": 2 * x + 1 - c}
    nxt, prv = {"tensor": 2 * xp + c}, {"tensor": 2 * xm + c}
    pair = {"dp": 1 - dp}

    def head_peer(k):
        return {"head": lax.rem(h + k, nh)}

    barrier = pltpu.get_barrier_semaphore()
    partners = [sib, nxt, prv, pair] + [head_peer(k) for k in range(1, nh)]
    for partner in partners:
        pl.semaphore_signal(barrier, inc=1, device_id=partner, device_id_type=MESH)

    def local(src, dst, sem):
        return pltpu.make_async_copy(src, dst, sem)

    def small_loads():
        return [
            local(r.tokens, r.tok, r.small_sem.at[0]),
            local(r.cotangent, r.cot, r.small_sem.at[1]),
            local(r.routes, r.rts, r.small_sem.at[2]),
            local(r.heads, r.hup, r.small_sem.at[3]),
            local(r.factor, r.cdf, r.small_sem.at[4]),
        ]

    def chunk_loads(j):
        rows = pl.ds(pl.multiple_of(j * CHUNK, CHUNK), CHUNK)
        return [
            local(r.w_gate.at[rows, :], r.wgu.at[j, pl.ds(0, CHUNK), :], r.load_sem.at[j, 0]),
            local(r.w_up.at[rows, :], r.wgu.at[j, pl.ds(CHUNK, CHUNK), :], r.load_sem.at[j, 1]),
            local(r.w_down.at[rows, :], r.wd.at[j], r.load_sem.at[j, 2]),
        ]

    def tail_loads():
        rows = pl.ds(hidden, tail)
        return [
            local(r.w_gate.at[rows, :], r.t_wgu.at[pl.ds(0, tail), :], r.small_sem.at[5]),
            local(r.w_up.at[rows, :], r.t_wgu.at[pl.ds(TAIL, tail), :], r.small_sem.at[6]),
            local(r.w_down.at[rows, :], r.t_wd.at[pl.ds(0, tail), :], r.small_sem.at[7]),
        ]

    first = small_loads()
    first[0].start()
    for load in chunk_loads(0):
        load.start()
    for load in first[1:]:
        load.start()
    r.t_wgu[...] = jnp.zeros_like(r.t_wgu)
    r.t_wd[...] = jnp.zeros_like(r.t_wd)
    for load in tail_loads():
        load.start()

    def start_chunk(j, carry):
        for load in chunk_loads(j):
            load.start()
        return carry

    lax.fori_loop(1, nj, start_chunk, 0)

    def main():
        b = Box()
        b.part, b.sibs = r.m_part, r.m_sibs
        b.s1, b.s2, b.s3, b.r1, b.r2, b.r3 = r.m_s1, r.m_s2, r.m_s3, r.m_r1, r.m_r2, r.m_r3
        b.grads, b.send, b.recv, b.width = r.m_grads, r.m_send, r.m_recv, CHUNK
        return b

    def special():
        b = Box()
        b.part, b.sibs = r.t_part, r.t_sibs
        b.s1, b.s2, b.s3, b.r1, b.r2, b.r3 = r.t_s1, r.t_s2, r.t_s3, r.t_r1, r.t_r2, r.t_r3
        b.grads, b.send, b.recv, b.width = r.t_grads, r.t_send, r.t_recv, TAIL
        return b

    main, special = main(), special()

    def remote(b, j, i, src, dst, to):
        return pltpu.make_async_remote_copy(
            src_ref=src,
            dst_ref=dst,
            send_sem=b.send.at[j, i],
            recv_sem=b.recv.at[j, i],
            device_id=to,
            device_id_type=MESH,
        )

    def to_sib(b, j):
        return remote(b, j, 0, b.part.at[j, 1 - c], b.sibs.at[j], sib)

    def sum_far(b, j):
        return remote(b, j, 1, b.s1.at[j], b.r1.at[j], nxt)

    def sum_near(b, j):
        return remote(b, j, 2, b.s2.at[j], b.r2.at[j], prv)

    def sum_on(b, j):
        return remote(b, j, 3, b.s3.at[j], b.r3.at[j], nxt)

    def grad(b, j, i, slot, to):
        return remote(b, j, i, b.grads.at[j, slot], b.grads.at[j, slot], to)

    own, far, near, ahead = 2 * x + c, 2 * x2 + c, 2 * xm + c, 2 * xp + c
    sib_own, sib_far, sib_near, sib_ahead = (
        2 * x + 1 - c,
        2 * x2 + 1 - c,
        2 * xm + 1 - c,
        2 * xp + 1 - c,
    )

    def add(b, j):
        to_sib(b, j).wait_recv()
        b.s1[j] = (b.part[j, c, x2].astype(F32) + b.sibs[j, x2].astype(F32)).astype(BF16)
        sum_far(b, j).start()
        b.s2[j] = (b.part[j, c, xm].astype(F32) + b.sibs[j, xm].astype(F32)).astype(BF16)
        sum_near(b, j).start()

    def relay(b, j):
        sum_far(b, j).wait_recv()
        b.s3[j] = (
            b.r1[j].astype(F32) + b.part[j, c, xp].astype(F32) + b.sibs[j, xp].astype(F32)
        ).astype(BF16)
        sum_on(b, j).start()

    def totals(b, j):
        sum_near(b, j).wait_recv()
        sum_on(b, j).wait_recv()
        width = b.width

        def part(lo, size):
            at = pl.ds(lo, size)
            return (
                b.r3[j, :, at].astype(F32)
                + b.r2[j, :, at].astype(F32)
                + b.part[j, c, x, :, at].astype(F32)
                + b.sibs[j, x, :, at].astype(F32)
            )

        gate, up, back = (part(i * width, width) for i in range(3))
        sig = jax.nn.sigmoid(gate)
        b.grads[j, own, :, pl.ds(0, width)] = (
            back * up * sig * (1.0 + gate * (1.0 - sig))
        ).astype(BF16)
        b.grads[j, own, :, pl.ds(width, width)] = (back * gate * sig).astype(BF16)
        return part

    def spread(b, j):
        grad(b, j, 4, own, nxt).start()
        grad(b, j, 5, own, prv).start()
        grad(b, j, 6, own, sib).start()

    def forward(b, j):
        grad(b, j, 4, near, nxt).wait_recv()
        grad(b, j, 7, near, nxt).start()
        grad(b, j, 8, near, sib).start()
        grad(b, j, 5, ahead, prv).wait_recv()
        grad(b, j, 9, ahead, sib).start()

    def last(b, j):
        grad(b, j, 7, far, nxt).wait_recv()
        grad(b, j, 10, far, sib).start()

    def arrived(b, j):
        grad(b, j, 6, sib_own, sib).wait_recv()
        grad(b, j, 8, sib_ahead, sib).wait_recv()
        grad(b, j, 9, sib_near, sib).wait_recv()
        grad(b, j, 10, sib_far, sib).wait_recv()

    def all_sent(b, j):
        for copy in (to_sib(b, j), sum_far(b, j), sum_near(b, j), sum_on(b, j)):
            copy.wait_send()
        grad(b, j, 4, own, nxt).wait_send()
        grad(b, j, 5, own, prv).wait_send()
        grad(b, j, 6, own, sib).wait_send()
        grad(b, j, 7, near, nxt).wait_send()
        grad(b, j, 8, near, sib).wait_send()
        grad(b, j, 9, ahead, sib).wait_send()
        grad(b, j, 10, far, sib).wait_send()

    def store_part(b, j, lo, value):
        for q in range(4):
            for core in range(2):
                at = (2 * q + core) * 32
                b.part[j, core, q, :, pl.ds(lo, value.shape[1])] = value[at : at + 32].astype(BF16)

    def other(i, src, dst, to):
        return pltpu.make_async_remote_copy(
            src_ref=src,
            dst_ref=dst,
            send_sem=r.o_send.at[i],
            recv_sem=r.o_recv.at[i],
            device_id=to,
            device_id_type=MESH,
        )

    def pair_cot():
        return other(0, r.cot, r.p_cot, pair)

    def pair_routes():
        return other(1, r.rb, r.p_rb, pair)

    def pair_codes():
        return other(2, r.codes, r.p_codes, pair)

    def pair_shared():
        return other(3, r.shared, r.p_shared, pair)

    def code_copy(k):
        return other(4 + k, r.mine, r.hx.at[k], head_peer(k))

    def x_copy(k):
        return other(4 + nh + k, r.xs.at[k], r.xr.at[k], head_peer(k))

    first_head = h * r.hup.shape[0]
    rank = r.cdf.shape[0]

    def lanes(shape):
        return lax.broadcasted_iota(jnp.int32, shape, 1)

    def special_matmuls():
        for load in small_loads()[2:] + tail_loads():
            load.wait()
        factor = r.cdf[...]
        upper = jnp.concatenate([jnp.zeros_like(factor), factor], axis=0)
        tok, cot = r.tok[...], r.cot[...]
        store_part(special, 0, 0, nt(tok, r.t_wgu[...]))
        store_part(special, 0, 2 * TAIL, nt(cot, r.t_wd[...]))
        codes = nt(tok, upper)
        row = r.rts[...].astype(F32)
        routes = jnp.broadcast_to(row, (2 * rank, row.shape[1])).T
        r.rb[...] = routes.astype(BF16)
        pair_routes().start()
        total = jnp.zeros_like(codes)
        half = (lanes(codes.shape) >= rank).astype(F32)
        base = first_head.astype(F32) + half
        for p in range(r.hup.shape[0] // 2):
            flat = jnp.concatenate([r.hup[2 * p], r.hup[2 * p + 1]], axis=0)
            total += jnp.where(routes == base + 2.0 * p, nt(cot, flat), 0.0)
        total = ADAPTER_SCALE * (total + pltpu.roll(total, rank, 1))
        store_part(special, 0, 3 * TAIL, jnp.where(half == 0.0, total, codes))

    def special_totals():
        part = totals(special, 0)
        r.mine[...] = part(3 * TAIL, TAIL).astype(BF16)
        for k in range(1, nh):
            code_copy(k).start()

    def special_spread():
        mine = r.mine[...].astype(F32)
        total = mine
        for k in range(1, nh):
            code_copy(k).wait_recv()
            total += r.hx[k].astype(F32)
        total = jnp.where(lanes(mine.shape) < rank, total, mine)
        special.grads[0, own, :, pl.ds(2 * TAIL, TAIL)] = total.astype(BF16)
        spread(special, 0)

    def heads_out(p):
        at = pl.ds(2 * p, 2)
        return local(r.up16.at[at], r.o_heads.at[at], r.out_sem.at[p])

    def shared_out():
        return local(r.total, r.o_shared, r.out_sem.at[r.hup.shape[0] // 2])

    def up_heads(codes, routes, cot, fresh):
        both = jnp.where(
            lanes(codes.shape) < rank, pltpu.roll(codes.astype(F32), rank, 1), codes.astype(F32)
        )
        half = (lanes(codes.shape) >= rank).astype(F32)
        base = first_head.astype(F32) + half
        for p in range(r.hup.shape[0] // 2):
            chosen = jnp.where(routes.astype(F32) == base + 2.0 * p, both, 0.0).astype(BF16)
            grads = (ADAPTER_SCALE * tn(chosen, cot)).reshape(2, rank, cot.shape[1])
            if fresh:
                r.uph[pl.ds(2 * p, 2)] = grads
            else:
                r.up16[pl.ds(2 * p, 2)] = (r.uph[pl.ds(2 * p, 2)] + grads).astype(BF16)
                heads_out(p).start()

    def special_back():
        arrived(special, 0)
        grads = special.grads[0, :, :, pl.ds(0, 2 * TAIL)].reshape(256, 2 * TAIL)
        r.acc[...] = jnp.dot(grads, r.t_wgu[...], preferred_element_type=F32)
        codes = special.grads[0, :, :, pl.ds(2 * TAIL, TAIL)].reshape(256, TAIL)
        r.codes[...] = codes
        pair_codes().start()
        r.shared[...] = tn(codes, r.tok[...])[:rank].astype(BF16)
        pair_shared().start()
        up_heads(codes, r.rb[...], r.cot[...], True)
        mine = special.grads[0, h, :, pl.ds(2 * TAIL, TAIL)]
        factor = r.cdf[...]
        lower = jnp.concatenate([factor, jnp.zeros_like(factor)], axis=0)
        r.xcode[...] = jnp.dot(mine, lower, preferred_element_type=F32)

    def special_pair():
        pair_cot().wait_recv()
        pair_routes().wait_recv()
        pair_codes().wait_recv()
        up_heads(r.p_codes[...], r.p_rb[...], r.p_cot[...], False)
        pair_shared().wait_recv()
        r.total[...] = r.shared[...].astype(F32) + r.p_shared[...].astype(F32)
        shared_out().start()

    def matmuls(j):
        loads = chunk_loads(j)
        loads[0].wait()
        tok = r.tok[...]
        store_part(main, j, 0, nt(tok, r.wgu[j, pl.ds(0, CHUNK), :]))
        loads[1].wait()
        store_part(main, j, CHUNK, nt(tok, r.wgu[j, pl.ds(CHUNK, CHUNK), :]))
        loads[2].wait()
        store_part(main, j, 2 * CHUNK, nt(r.cot[...], r.wd[j]))

    def back(j):
        arrived(main, j)
        grads = main.grads[j].reshape(256, 2 * CHUNK)
        for n in range(2):
            at = pl.ds(n * 512, 512)
            r.acc[:, at] += jnp.dot(grads, r.wgu[j, :, at], preferred_element_type=F32)

    for load in small_loads()[:2]:
        load.wait()
    pl.semaphore_wait(barrier, len(partners))
    pair_cot().start()

    def tick(t, carry):
        def stage(lag, run):
            @pl.when((t >= lag) & (t < nj + lag))
            def _():
                run(t - lag)

        def once(at, run):
            pl.when(t == at)(run)

        def matmul_stage(j):
            matmuls(j)
            to_sib(main, j).start()

        def special_matmul_stage():
            special_matmuls()
            to_sib(special, 0).start()

        def grad_stage(j):
            totals(main, j)
            spread(main, j)

        stage(0, matmul_stage)
        once(0, special_matmul_stage)
        stage(LAG_ADD, lambda j: add(main, j))
        once(LAG_ADD, lambda: add(special, 0))
        stage(LAG_RELAY, lambda j: relay(main, j))
        once(LAG_RELAY, lambda: relay(special, 0))
        stage(LAG_GRAD, grad_stage)
        once(LAG_GRAD, special_totals)
        once(LAG_GRAD + 1, special_spread)
        stage(LAG_FORWARD, lambda j: forward(main, j))
        once(LAG_FORWARD + 1, lambda: forward(special, 0))
        stage(LAG_LAST, lambda j: last(main, j))
        once(LAG_LAST + 1, lambda: last(special, 0))
        once(LAG_BACK, special_back)
        stage(LAG_BACK, back)
        once(LAG_BACK + 4, special_pair)
        return carry

    lax.fori_loop(0, nj + LAG_BACK, tick, 0)

    for k in range(1, nh):
        rows = pl.ds(pl.multiple_of(lax.rem(h + k, nh) * 32, 32), 32)
        r.xs[k] = r.acc[rows, :].astype(BF16)
        x_copy(k).start()
    total = r.acc[pl.ds(pl.multiple_of(h * 32, 32), 32), :] + r.xcode[...]
    for k in range(1, nh):
        x_copy(k).wait_recv()
        total += r.xr[k].astype(F32)
    r.o_x[...] = total.astype(BF16)

    def sent(j, carry):
        all_sent(main, j)
        return carry

    lax.fori_loop(0, nj, sent, 0)
    all_sent(special, 0)
    for p in range(r.hup.shape[0] // 2):
        heads_out(p).wait()
    shared_out().wait()
    for copy in (pair_cot(), pair_routes(), pair_codes(), pair_shared()):
        copy.wait_send()
    for k in range(1, nh):
        code_copy(k).wait_send()
        x_copy(k).wait_send()


def finish(x_in, shared_in, heads_in, x_out, shared_out, heads_out, x, shared, half, heads, came, left):
    count = heads_in.shape[0]

    def heads_read(e):
        return pltpu.make_async_copy(heads_in.at[e], half.at[e], came.at[e])

    def heads_write(e):
        return pltpu.make_async_copy(heads.at[e], heads_out.at[e], left.at[e])

    steps = [(shared_in, shared, shared_out), (x_in, x, x_out)]
    reads = [pltpu.make_async_copy(a, b, came.at[count + i]) for i, (a, b, _) in enumerate(steps)]
    writes = [pltpu.make_async_copy(b, c, left.at[count + i]) for i, (_, b, c) in enumerate(steps)]
    for e in range(count):
        heads_read(e).start()
    for read in reads:
        read.start()
    for e in range(count):
        heads_read(e).wait()
        heads[e] = half[e].astype(F32)
        heads_write(e).start()
    for read, write in zip(reads, writes):
        read.wait()
        write.start()
    for e in range(count):
        heads_write(e).wait()
    for write in writes:
        write.wait()


def solution(mesh):
    nh = mesh.shape["head"]

    def step(tokens, cotangent, w_gate, w_up, w_down, factor, heads, routes):
        rows, width = tokens.shape
        w_gate, w_up, factor, routes = w_gate.T, w_up.T, factor.T, routes.T
        nj = w_gate.shape[0] // CHUNK
        rank, count = factor.shape[0], heads.shape[0]
        shapes = {}

        def vmem(name, shape, dtype=BF16):
            shapes[name] = pltpu.VMEM(shape, dtype)

        vmem("tok", (rows, width))
        vmem("cot", (rows, width))
        vmem("p_cot", (rows, width))
        vmem("rts", (1, rows), jnp.int32)
        vmem("hup", (count, rank, width))
        vmem("cdf", (rank, width))
        vmem("wgu", (nj, 2 * CHUNK, width))
        vmem("wd", (nj, CHUNK, width))
        vmem("t_wgu", (2 * TAIL, width))
        vmem("t_wd", (TAIL, width))
        for kind, n, unit, extra in (("m", nj, CHUNK, 0), ("t", 1, TAIL, TAIL)):
            full = 3 * unit + extra
            vmem(kind + "_part", (n, 2, 4, 32, full))
            vmem(kind + "_sibs", (n, 4, 32, full))
            for name in ("s1", "s2", "s3", "r1", "r2", "r3"):
                vmem(kind + "_" + name, (n, 32, full))
            vmem(kind + "_grads", (n, 8, 32, 2 * unit + extra))
            shapes[kind + "_send"] = pltpu.SemaphoreType.DMA((n, 11))
            shapes[kind + "_recv"] = pltpu.SemaphoreType.DMA((n, 11))
        vmem("rb", (rows, 2 * rank))
        vmem("p_rb", (rows, 2 * rank))
        vmem("codes", (rows, 2 * rank))
        vmem("p_codes", (rows, 2 * rank))
        vmem("shared", (rank, width))
        vmem("p_shared", (rank, width))
        vmem("mine", (32, 2 * rank))
        vmem("hx", (nh, 32, 2 * rank))
        vmem("xs", (nh, 32, width))
        vmem("xr", (nh, 32, width))
        vmem("acc", (rows, width), F32)
        vmem("xcode", (32, width), F32)
        vmem("uph", (count, rank, width), F32)
        vmem("up16", (count, rank, width))
        vmem("total", (rank, width), F32)
        shapes["o_send"] = pltpu.SemaphoreType.DMA((4 + 2 * nh,))
        shapes["o_recv"] = pltpu.SemaphoreType.DMA((4 + 2 * nh,))
        shapes["out_sem"] = pltpu.SemaphoreType.DMA((count // 2 + 1,))
        shapes["small_sem"] = pltpu.SemaphoreType.DMA((8,))
        shapes["load_sem"] = pltpu.SemaphoreType.DMA((nj, 3))
        names = ["tokens", "cotangent", "w_gate", "w_up", "w_down", "factor", "heads", "routes"]
        names += ["o_x", "o_shared", "o_heads"] + list(shapes)

        def kernel(*refs):
            body(names, nj, nh, *refs)

        any_space = pl.BlockSpec(memory_space=pl.ANY)
        made = pl.pallas_call(
            kernel,
            out_shape=(
                jax.ShapeDtypeStruct((32, width), BF16),
                jax.ShapeDtypeStruct((rank, width), F32),
                jax.ShapeDtypeStruct((count, rank, width), BF16),
            ),
            in_specs=[any_space] * 8,
            out_specs=(
                pl.BlockSpec(memory_space=pltpu.VMEM),
                any_space,
                any_space,
            ),
            scratch_shapes=list(shapes.values()),
            compiler_params=pltpu.CompilerParams(
                collective_id=0, has_side_effects=True, vmem_limit_bytes=60 * 1024 * 1024
            ),
            name="ffn_backward",
        )(tokens, cotangent, w_gate, w_up, w_down, factor, heads, routes)
        grad_x, shared, up = pl.pallas_call(
            finish,
            out_shape=(
                jax.ShapeDtypeStruct(made[0].shape, BF16),
                jax.ShapeDtypeStruct(made[1].shape, F32),
                jax.ShapeDtypeStruct(made[2].shape, F32),
            ),
            in_specs=[any_space] * 3,
            out_specs=(any_space,) * 3,
            scratch_shapes=[pltpu.VMEM(m.shape, m.dtype) for m in made]
            + [pltpu.VMEM(made[2].shape, F32)]
            + [pltpu.SemaphoreType.DMA((count + 2,))] * 2,
            name="write_out",
        )(*made)
        return grad_x, shared.T, up

    placed = (
        P("dp", "tensor"),
        P("dp", "tensor"),
        P("tensor", "head"),
        P("tensor", "head"),
        P("head", "tensor"),
        P("tensor", None),
        P("head", None, "tensor"),
        P("dp", None),
    )
    return jax.shard_map(
        step,
        mesh=mesh,
        in_specs=placed,
        out_specs=(P(("dp", "head"), "tensor"), P("tensor", None), P("head", None, "tensor")),
        check_vma=False,
    )
```

```python
import jax
import jax.numpy as jnp
from jax import lax
from jax.experimental import pallas as pl
from jax.experimental.pallas import tpu as pltpu
from jax.sharding import PartitionSpec as P

ADAPTER_SCALE = 2.0
MESH = pl.DeviceIdType.MESH
F32, BF16 = jnp.float32, jnp.bfloat16
CHUNK = 512
TAIL = 128
LAG_ADD, LAG_RELAY, LAG_GRAD, LAG_FORWARD, LAG_LAST, LAG_BACK = 1, 3, 5, 7, 9, 11


class Box:
    pass


def nt(left, right):
    return lax.dot_general(left, right, (((1,), (1,)), ((), ())), preferred_element_type=F32)


def tn(left, right):
    return lax.dot_general(left, right, (((0,), (0,)), ((), ())), preferred_element_type=F32)


def body(names, nj, nh, *refs):
    r = Box()
    for name, ref in zip(names, refs):
        setattr(r, name, ref)
    hidden = nj * CHUNK
    tail = r.w_gate.shape[0] - hidden
    tau, h, dp = lax.axis_index("tensor"), lax.axis_index("head"), lax.axis_index("dp")
    x, c = tau // 2, lax.rem(tau, 2)
    step = 2 * c - 1
    xp, xm, x2 = lax.rem(x + step + 4, 4), lax.rem(x - step + 4, 4), lax.rem(x + 2, 4)
    sib = {"tensor": 2 * x + 1 - c}
    nxt, prv = {"tensor": 2 * xp + c}, {"tensor": 2 * xm + c}
    pair = {"dp": 1 - dp}

    def head_peer(k):
        return {"head": lax.rem(h + k, nh)}

    barrier = pltpu.get_barrier_semaphore()
    partners = [sib, nxt, prv, pair] + [head_peer(k) for k in range(1, nh)]
    for partner in partners:
        pl.semaphore_signal(barrier, inc=1, device_id=partner, device_id_type=MESH)

    def local(src, dst, sem):
        return pltpu.make_async_copy(src, dst, sem)

    def small_loads():
        return [
            local(r.tokens, r.tok, r.small_sem.at[0]),
            local(r.cotangent, r.cot, r.small_sem.at[1]),
            local(r.routes, r.rts, r.small_sem.at[2]),
            local(r.heads, r.hup, r.small_sem.at[3]),
            local(r.factor, r.cdf, r.small_sem.at[4]),
        ]

    def chunk_loads(j):
        rows = pl.ds(pl.multiple_of(j * CHUNK, CHUNK), CHUNK)
        return [
            local(r.w_gate.at[rows, :], r.wgu.at[j, pl.ds(0, CHUNK), :], r.load_sem.at[j, 0]),
            local(r.w_up.at[rows, :], r.wgu.at[j, pl.ds(CHUNK, CHUNK), :], r.load_sem.at[j, 1]),
            local(r.w_down.at[rows, :], r.wd.at[j], r.load_sem.at[j, 2]),
        ]

    def tail_loads():
        rows = pl.ds(hidden, tail)
        return [
            local(r.w_gate.at[rows, :], r.t_wgu.at[pl.ds(0, tail), :], r.small_sem.at[5]),
            local(r.w_up.at[rows, :], r.t_wgu.at[pl.ds(TAIL, tail), :], r.small_sem.at[6]),
            local(r.w_down.at[rows, :], r.t_wd.at[pl.ds(0, tail), :], r.small_sem.at[7]),
        ]

    first = small_loads()
    first[0].start()
    for load in chunk_loads(0):
        load.start()
    for load in first[1:]:
        load.start()
    r.t_wgu[...] = jnp.zeros_like(r.t_wgu)
    r.t_wd[...] = jnp.zeros_like(r.t_wd)
    for load in tail_loads():
        load.start()

    def start_chunk(j, carry):
        for load in chunk_loads(j):
            load.start()
        return carry

    lax.fori_loop(1, nj, start_chunk, 0)

    def main():
        b = Box()
        b.part, b.sibs = r.m_part, r.m_sibs
        b.s1, b.s2, b.s3, b.r1, b.r2, b.r3 = r.m_s1, r.m_s2, r.m_s3, r.m_r1, r.m_r2, r.m_r3
        b.grads, b.send, b.recv, b.width = r.m_grads, r.m_send, r.m_recv, CHUNK
        return b

    def special():
        b = Box()
        b.part, b.sibs = r.t_part, r.t_sibs
        b.s1, b.s2, b.s3, b.r1, b.r2, b.r3 = r.t_s1, r.t_s2, r.t_s3, r.t_r1, r.t_r2, r.t_r3
        b.grads, b.send, b.recv, b.width = r.t_grads, r.t_send, r.t_recv, TAIL
        return b

    main, special = main(), special()

    def remote(b, j, i, src, dst, to):
        return pltpu.make_async_remote_copy(
            src_ref=src,
            dst_ref=dst,
            send_sem=b.send.at[j, i],
            recv_sem=b.recv.at[j, i],
            device_id=to,
            device_id_type=MESH,
        )

    def to_sib(b, j):
        return remote(b, j, 0, b.part.at[j, 1 - c], b.sibs.at[j], sib)

    def sum_far(b, j):
        return remote(b, j, 1, b.s1.at[j], b.r1.at[j], nxt)

    def sum_near(b, j):
        return remote(b, j, 2, b.s2.at[j], b.r2.at[j], prv)

    def sum_on(b, j):
        return remote(b, j, 3, b.s3.at[j], b.r3.at[j], nxt)

    def grad(b, j, i, slot, to):
        return remote(b, j, i, b.grads.at[j, slot], b.grads.at[j, slot], to)

    own, far, near, ahead = 2 * x + c, 2 * x2 + c, 2 * xm + c, 2 * xp + c
    sib_own, sib_far, sib_near, sib_ahead = (
        2 * x + 1 - c,
        2 * x2 + 1 - c,
        2 * xm + 1 - c,
        2 * xp + 1 - c,
    )

    def add(b, j):
        to_sib(b, j).wait_recv()
        b.s1[j] = (b.part[j, c, x2].astype(F32) + b.sibs[j, x2].astype(F32)).astype(BF16)
        sum_far(b, j).start()
        b.s2[j] = (b.part[j, c, xm].astype(F32) + b.sibs[j, xm].astype(F32)).astype(BF16)
        sum_near(b, j).start()

    def relay(b, j):
        sum_far(b, j).wait_recv()
        b.s3[j] = (
            b.r1[j].astype(F32) + b.part[j, c, xp].astype(F32) + b.sibs[j, xp].astype(F32)
        ).astype(BF16)
        sum_on(b, j).start()

    def totals(b, j):
        sum_near(b, j).wait_recv()
        sum_on(b, j).wait_recv()
        width = b.width

        def part(lo, size):
            at = pl.ds(lo, size)
            return (
                b.r3[j, :, at].astype(F32)
                + b.r2[j, :, at].astype(F32)
                + b.part[j, c, x, :, at].astype(F32)
                + b.sibs[j, x, :, at].astype(F32)
            )

        gate, up, back = (part(i * width, width) for i in range(3))
        sig = jax.nn.sigmoid(gate)
        b.grads[j, own, :, pl.ds(0, width)] = (
            back * up * sig * (1.0 + gate * (1.0 - sig))
        ).astype(BF16)
        b.grads[j, own, :, pl.ds(width, width)] = (back * gate * sig).astype(BF16)
        return part

    def spread(b, j):
        grad(b, j, 4, own, nxt).start()
        grad(b, j, 5, own, prv).start()
        grad(b, j, 6, own, sib).start()

    def forward(b, j):
        grad(b, j, 4, near, nxt).wait_recv()
        grad(b, j, 7, near, nxt).start()
        grad(b, j, 8, near, sib).start()
        grad(b, j, 5, ahead, prv).wait_recv()
        grad(b, j, 9, ahead, sib).start()

    def last(b, j):
        grad(b, j, 7, far, nxt).wait_recv()
        grad(b, j, 10, far, sib).start()

    def arrived(b, j):
        grad(b, j, 6, sib_own, sib).wait_recv()
        grad(b, j, 8, sib_ahead, sib).wait_recv()
        grad(b, j, 9, sib_near, sib).wait_recv()
        grad(b, j, 10, sib_far, sib).wait_recv()

    def all_sent(b, j):
        for copy in (to_sib(b, j), sum_far(b, j), sum_near(b, j), sum_on(b, j)):
            copy.wait_send()
        grad(b, j, 4, own, nxt).wait_send()
        grad(b, j, 5, own, prv).wait_send()
        grad(b, j, 6, own, sib).wait_send()
        grad(b, j, 7, near, nxt).wait_send()
        grad(b, j, 8, near, sib).wait_send()
        grad(b, j, 9, ahead, sib).wait_send()
        grad(b, j, 10, far, sib).wait_send()

    def store_part(b, j, lo, value):
        for q in range(4):
            for core in range(2):
                at = (2 * q + core) * 32
                b.part[j, core, q, :, pl.ds(lo, value.shape[1])] = value[at : at + 32].astype(BF16)

    def other(i, src, dst, to):
        return pltpu.make_async_remote_copy(
            src_ref=src,
            dst_ref=dst,
            send_sem=r.o_send.at[i],
            recv_sem=r.o_recv.at[i],
            device_id=to,
            device_id_type=MESH,
        )

    def pair_cot():
        return other(0, r.cot, r.p_cot, pair)

    def pair_routes():
        return other(1, r.rb, r.p_rb, pair)

    def pair_codes():
        return other(2, r.codes, r.p_codes, pair)

    def pair_shared():
        return other(3, r.shared, r.p_shared, pair)

    def code_copy(k):
        return other(4 + k, r.mine, r.hx.at[k], head_peer(k))

    def x_copy(k):
        return other(4 + nh + k, r.xs.at[k], r.xr.at[k], head_peer(k))

    first_head = h * r.hup.shape[0]
    rank = r.cdf.shape[0]

    def lanes(shape):
        return lax.broadcasted_iota(jnp.int32, shape, 1)

    def special_matmuls():
        for load in small_loads()[2:] + tail_loads():
            load.wait()
        factor = r.cdf[...]
        upper = jnp.concatenate([jnp.zeros_like(factor), factor], axis=0)
        tok, cot = r.tok[...], r.cot[...]
        store_part(special, 0, 0, nt(tok, r.t_wgu[...]))
        store_part(special, 0, 2 * TAIL, nt(cot, r.t_wd[...]))
        codes = nt(tok, upper)
        row = r.rts[...].astype(F32)
        routes = jnp.broadcast_to(row, (2 * rank, row.shape[1])).T
        r.rb[...] = routes.astype(BF16)
        pair_routes().start()
        total = jnp.zeros_like(codes)
        half = (lanes(codes.shape) >= rank).astype(F32)
        base = first_head.astype(F32) + half
        for p in range(r.hup.shape[0] // 2):
            flat = jnp.concatenate([r.hup[2 * p], r.hup[2 * p + 1]], axis=0)
            total += jnp.where(routes == base + 2.0 * p, nt(cot, flat), 0.0)
        total = ADAPTER_SCALE * (total + pltpu.roll(total, rank, 1))
        store_part(special, 0, 3 * TAIL, jnp.where(half == 0.0, total, codes))

    def special_totals():
        part = totals(special, 0)
        r.mine[...] = part(3 * TAIL, TAIL).astype(BF16)
        for k in range(1, nh):
            code_copy(k).start()

    def special_spread():
        mine = r.mine[...].astype(F32)
        total = mine
        for k in range(1, nh):
            code_copy(k).wait_recv()
            total += r.hx[k].astype(F32)
        total = jnp.where(lanes(mine.shape) < rank, total, mine)
        special.grads[0, own, :, pl.ds(2 * TAIL, TAIL)] = total.astype(BF16)
        spread(special, 0)

    def heads_out(p):
        at = pl.ds(2 * p, 2)
        return local(r.up16.at[at], r.o_heads.at[at], r.out_sem.at[p])

    def shared_out():
        return local(r.total, r.o_shared, r.out_sem.at[r.hup.shape[0] // 2])

    def up_heads(codes, routes, cot, fresh):
        both = jnp.where(
            lanes(codes.shape) < rank, pltpu.roll(codes.astype(F32), rank, 1), codes.astype(F32)
        )
        half = (lanes(codes.shape) >= rank).astype(F32)
        base = first_head.astype(F32) + half
        for p in range(r.hup.shape[0] // 2):
            chosen = jnp.where(routes.astype(F32) == base + 2.0 * p, both, 0.0).astype(BF16)
            grads = (ADAPTER_SCALE * tn(chosen, cot)).reshape(2, rank, cot.shape[1])
            if fresh:
                r.uph[pl.ds(2 * p, 2)] = grads
            else:
                r.up16[pl.ds(2 * p, 2)] = (r.uph[pl.ds(2 * p, 2)] + grads).astype(BF16)
                heads_out(p).start()

    def special_back():
        arrived(special, 0)
        grads = special.grads[0, :, :, pl.ds(0, 2 * TAIL)].reshape(256, 2 * TAIL)
        r.acc[...] = jnp.dot(grads, r.t_wgu[...], preferred_element_type=F32)
        codes = special.grads[0, :, :, pl.ds(2 * TAIL, TAIL)].reshape(256, TAIL)
        r.codes[...] = codes
        pair_codes().start()
        r.shared[...] = tn(codes, r.tok[...])[:rank].astype(BF16)
        pair_shared().start()
        up_heads(codes, r.rb[...], r.cot[...], True)
        mine = special.grads[0, h, :, pl.ds(2 * TAIL, TAIL)]
        factor = r.cdf[...]
        lower = jnp.concatenate([factor, jnp.zeros_like(factor)], axis=0)
        r.xcode[...] = jnp.dot(mine, lower, preferred_element_type=F32)

    def special_pair():
        pair_cot().wait_recv()
        pair_routes().wait_recv()
        pair_codes().wait_recv()
        up_heads(r.p_codes[...], r.p_rb[...], r.p_cot[...], False)
        pair_shared().wait_recv()
        r.total[...] = r.shared[...].astype(F32) + r.p_shared[...].astype(F32)
        shared_out().start()

    def matmuls(j):
        loads = chunk_loads(j)
        loads[0].wait()
        tok = r.tok[...]
        store_part(main, j, 0, nt(tok, r.wgu[j, pl.ds(0, CHUNK), :]))
        loads[1].wait()
        store_part(main, j, CHUNK, nt(tok, r.wgu[j, pl.ds(CHUNK, CHUNK), :]))
        loads[2].wait()
        store_part(main, j, 2 * CHUNK, nt(r.cot[...], r.wd[j]))

    def back(j):
        arrived(main, j)
        grads = main.grads[j].reshape(256, 2 * CHUNK)
        for n in range(2):
            at = pl.ds(n * 512, 512)
            r.acc[:, at] += jnp.dot(grads, r.wgu[j, :, at], preferred_element_type=F32)

    for load in small_loads()[:2]:
        load.wait()
    pl.semaphore_wait(barrier, len(partners))
    pair_cot().start()

    def tick(t, carry):
        def stage(lag, run):
            @pl.when((t >= lag) & (t < nj + lag))
            def _():
                run(t - lag)

        def once(at, run):
            pl.when(t == at)(run)

        def matmul_stage(j):
            matmuls(j)
            to_sib(main, j).start()

        def special_matmul_stage():
            special_matmuls()
            to_sib(special, 0).start()

        def grad_stage(j):
            totals(main, j)
            spread(main, j)

        stage(0, matmul_stage)
        stage(LAG_ADD, lambda j: add(main, j))
        once(LAG_ADD, special_matmul_stage)
        once(LAG_ADD + 1, lambda: add(special, 0))
        stage(LAG_RELAY, lambda j: relay(main, j))
        once(LAG_RELAY, lambda: relay(special, 0))
        stage(LAG_GRAD, grad_stage)
        once(LAG_GRAD, special_totals)
        once(LAG_GRAD + 1, special_spread)
        stage(LAG_FORWARD, lambda j: forward(main, j))
        once(LAG_FORWARD + 1, lambda: forward(special, 0))
        stage(LAG_LAST, lambda j: last(main, j))
        once(LAG_LAST + 1, lambda: last(special, 0))
        once(LAG_BACK, special_back)
        stage(LAG_BACK, back)
        once(LAG_BACK + 4, special_pair)
        return carry

    lax.fori_loop(0, nj + LAG_BACK, tick, 0)

    for k in range(1, nh):
        rows = pl.ds(pl.multiple_of(lax.rem(h + k, nh) * 32, 32), 32)
        r.xs[k] = r.acc[rows, :].astype(BF16)
        x_copy(k).start()
    total = r.acc[pl.ds(pl.multiple_of(h * 32, 32), 32), :] + r.xcode[...]
    for k in range(1, nh):
        x_copy(k).wait_recv()
        total += r.xr[k].astype(F32)
    r.o_x[...] = total.astype(BF16)

    def sent(j, carry):
        all_sent(main, j)
        return carry

    lax.fori_loop(0, nj, sent, 0)
    all_sent(special, 0)
    for p in range(r.hup.shape[0] // 2):
        heads_out(p).wait()
    shared_out().wait()
    for copy in (pair_cot(), pair_routes(), pair_codes(), pair_shared()):
        copy.wait_send()
    for k in range(1, nh):
        code_copy(k).wait_send()
        x_copy(k).wait_send()


def finish(x_in, shared_in, heads_in, x_out, shared_out, heads_out, x, shared, half, heads, came, left):
    count = heads_in.shape[0]

    def heads_read(e):
        return pltpu.make_async_copy(heads_in.at[e], half.at[e], came.at[e])

    def heads_write(e):
        return pltpu.make_async_copy(heads.at[e], heads_out.at[e], left.at[e])

    steps = [(shared_in, shared, shared_out), (x_in, x, x_out)]
    reads = [pltpu.make_async_copy(a, b, came.at[count + i]) for i, (a, b, _) in enumerate(steps)]
    writes = [pltpu.make_async_copy(b, c, left.at[count + i]) for i, (_, b, c) in enumerate(steps)]
    for e in range(count):
        heads_read(e).start()
    for read in reads:
        read.start()
    for e in range(count):
        heads_read(e).wait()
        heads[e] = half[e].astype(F32)
        heads_write(e).start()
    for read, write in zip(reads, writes):
        read.wait()
        write.start()
    for e in range(count):
        heads_write(e).wait()
    for write in writes:
        write.wait()


def solution(mesh):
    nh = mesh.shape["head"]

    def step(tokens, cotangent, w_gate, w_up, w_down, factor, heads, routes):
        rows, width = tokens.shape
        w_gate, w_up, factor, routes = w_gate.T, w_up.T, factor.T, routes.T
        nj = w_gate.shape[0] // CHUNK
        rank, count = factor.shape[0], heads.shape[0]
        shapes = {}

        def vmem(name, shape, dtype=BF16):
            shapes[name] = pltpu.VMEM(shape, dtype)

        vmem("tok", (rows, width))
        vmem("cot", (rows, width))
        vmem("p_cot", (rows, width))
        vmem("rts", (1, rows), jnp.int32)
        vmem("hup", (count, rank, width))
        vmem("cdf", (rank, width))
        vmem("wgu", (nj, 2 * CHUNK, width))
        vmem("wd", (nj, CHUNK, width))
        vmem("t_wgu", (2 * TAIL, width))
        vmem("t_wd", (TAIL, width))
        for kind, n, unit, extra in (("m", nj, CHUNK, 0), ("t", 1, TAIL, TAIL)):
            full = 3 * unit + extra
            vmem(kind + "_part", (n, 2, 4, 32, full))
            vmem(kind + "_sibs", (n, 4, 32, full))
            for name in ("s1", "s2", "s3", "r1", "r2", "r3"):
                vmem(kind + "_" + name, (n, 32, full))
            vmem(kind + "_grads", (n, 8, 32, 2 * unit + extra))
            shapes[kind + "_send"] = pltpu.SemaphoreType.DMA((n, 11))
            shapes[kind + "_recv"] = pltpu.SemaphoreType.DMA((n, 11))
        vmem("rb", (rows, 2 * rank))
        vmem("p_rb", (rows, 2 * rank))
        vmem("codes", (rows, 2 * rank))
        vmem("p_codes", (rows, 2 * rank))
        vmem("shared", (rank, width))
        vmem("p_shared", (rank, width))
        vmem("mine", (32, 2 * rank))
        vmem("hx", (nh, 32, 2 * rank))
        vmem("xs", (nh, 32, width))
        vmem("xr", (nh, 32, width))
        vmem("acc", (rows, width), F32)
        vmem("xcode", (32, width), F32)
        vmem("uph", (count, rank, width), F32)
        vmem("up16", (count, rank, width))
        vmem("total", (rank, width), F32)
        shapes["o_send"] = pltpu.SemaphoreType.DMA((4 + 2 * nh,))
        shapes["o_recv"] = pltpu.SemaphoreType.DMA((4 + 2 * nh,))
        shapes["out_sem"] = pltpu.SemaphoreType.DMA((count // 2 + 1,))
        shapes["small_sem"] = pltpu.SemaphoreType.DMA((8,))
        shapes["load_sem"] = pltpu.SemaphoreType.DMA((nj, 3))
        names = ["tokens", "cotangent", "w_gate", "w_up", "w_down", "factor", "heads", "routes"]
        names += ["o_x", "o_shared", "o_heads"] + list(shapes)

        def kernel(*refs):
            body(names, nj, nh, *refs)

        any_space = pl.BlockSpec(memory_space=pl.ANY)
        made = pl.pallas_call(
            kernel,
            out_shape=(
                jax.ShapeDtypeStruct((32, width), BF16),
                jax.ShapeDtypeStruct((rank, width), F32),
                jax.ShapeDtypeStruct((count, rank, width), BF16),
            ),
            in_specs=[any_space] * 8,
            out_specs=(
                pl.BlockSpec(memory_space=pltpu.VMEM),
                any_space,
                any_space,
            ),
            scratch_shapes=list(shapes.values()),
            compiler_params=pltpu.CompilerParams(
                collective_id=0, has_side_effects=True, vmem_limit_bytes=60 * 1024 * 1024
            ),
            name="ffn_backward",
        )(tokens, cotangent, w_gate, w_up, w_down, factor, heads, routes)
        grad_x, shared, up = pl.pallas_call(
            finish,
            out_shape=(
                jax.ShapeDtypeStruct(made[0].shape, BF16),
                jax.ShapeDtypeStruct(made[1].shape, F32),
                jax.ShapeDtypeStruct(made[2].shape, F32),
            ),
            in_specs=[any_space] * 3,
            out_specs=(any_space,) * 3,
            scratch_shapes=[pltpu.VMEM(m.shape, m.dtype) for m in made]
            + [pltpu.VMEM(made[2].shape, F32)]
            + [pltpu.SemaphoreType.DMA((count + 2,))] * 2,
            name="write_out",
        )(*made)
        return grad_x, shared.T, up

    placed = (
        P("dp", "tensor"),
        P("dp", "tensor"),
        P("tensor", "head"),
        P("tensor", "head"),
        P("head", "tensor"),
        P("tensor", None),
        P("head", None, "tensor"),
        P("dp", None),
    )
    return jax.shard_map(
        step,
        mesh=mesh,
        in_specs=placed,
        out_specs=(P(("dp", "head"), "tensor"), P("tensor", None), P("head", None, "tensor")),
        check_vma=False,
    )
```
